512 devices in a mesh: src: 32 (over z, x_lo), rcv: 8 (over y, x_hi), frq: 2 (over core).
Axes of the slice: x: 4 (x_hi: 2, x_lo: 2; x = x_hi * 2 + x_lo), y: 4, z: 16, core: 2. Of those that a mesh axis runs over, the one named last changes fastest.
Arguments:
- f_time: bfloat16 [512, 64, 8192], P('frq', 'src', 'rcv'), may hold values from -6 to 6
- reflect: bfloat16 [2, 8, 5888, 8192], P(None, 'frq', 'src', 'rcv'), may hold values from -0.0625 to 0.0625
- band_map: int32 [736, 32], P('src', 'rcv'), may hold values from 0 to 1, as said below
- gates: int32 [64], replicated, may hold values from 128 to 511
Outputs:
- focused: bfloat16 [512, 64, 8192], P('frq', 'src', 'rcv')
The draws below stay inside these ranges and needn't reach their ends.
Inputs may be any that keep to these rules, and one draw needn't show every extreme that they name: band_map[i, j] is 1 exactly where |j - ((2 i + 1) * 32) // 1472| is at most a half-width drawn for source block i between 8 and 16.
All inputs are finite; a program needn't handle non-finite values.
Results may differ from the reference program's by a relative error of at most 0.004.
The reference program's roundings to bfloat16 on the way count: a program that leaves them out, or rounds other values in their place, can miss the bound.
Values may be sent and summed in bfloat16 or wider, within the bound.
No kernel may reach another device: no remote copies, remote signals or barrier semaphores. Data moves between devices by JAX's collectives and lax.ppermute only.
A program may use at most 64 MiB of HBM per device.

```python
import math
import jax
import jax.numpy as jnp
from jax import lax

NT = 512
FREQ = 8
FOCAL = 64
NS = 5888
NR = 8192
NSB = 736
NRB = 32
SBLK = 8
RBLK = 256


def draw_band_map(key, part):
    row_index = jnp.arange(NSB, dtype=jnp.int32)
    col_index = jnp.arange(NRB, dtype=jnp.int32)
    centre_col = (2 * row_index + 1) * NRB // (2 * NSB)
    half_width = jax.random.randint(jax.random.fold_in(key, 11), (NSB,), NRB // 4, NRB // 2 + 1)
    inside = jnp.abs(col_index[None, :] - centre_col[:, None]) <= half_width[:, None]
    return inside.astype(jnp.int32)


def draw_gates(key, part):
    base_gates = jax.random.randint(jax.random.fold_in(key, 21), (FOCAL,), NT // 4, NT)
    order_ids = jax.random.permutation(jax.random.fold_in(key, 22), FOCAL)
    base_gates = base_gates.at[order_ids[0]].set(NT // 4)
    base_gates = base_gates.at[order_ids[1]].set(NT - 1)
    return base_gates.astype(jnp.int32)


def steps_of(rng, extent, pieces, low, high):
    level = 1.0
    for axis_at, blocks in pieces:
        draws = jax.random.uniform(jax.random.fold_in(jax.random.fold_in(rng, 6), axis_at), (blocks,), jnp.float32, low / len(pieces), high / len(pieces))
        level = level * jnp.repeat(jnp.exp(draws), extent[axis_at] // blocks).reshape((-1,) + (1,) * (len(extent) - 1 - axis_at))
    return level


def scatter_about(own_key, dims, width, bound, shards=(), kind=jnp.bfloat16):
    entries = jax.random.normal(own_key, dims, jnp.float32) * width
    if len(shards) > 0:
        entries = steps_of(own_key, dims, shards, -0.22, 0.18) * entries
    return jnp.clip(entries, min=-bound, max=bound).astype(kind)


def setup_inputs(seed: int = 0) -> dict:
    key_of = jax.random.split(jax.random.key(seed), 5)
    f_time = scatter_about(key_of[0], (NT, FOCAL, NR), 1.0, 6.0, ((0, 2), (1, 32), (2, 8)))
    reflect = scatter_about(key_of[1], (2, FREQ, NS, NR), NR ** -0.5, 0.0625, ((1, 2), (2, 32), (3, 8)))
    band_map = draw_band_map(jax.random.fold_in(key_of[4], 71), 0)
    gates = draw_gates(jax.random.fold_in(key_of[4], 71), 0)
    return dict(f_time=f_time, reflect=reflect, band_map=band_map, gates=gates)


def angle_table(sample_ids):
    freq_ids = jnp.arange(FREQ, dtype=jnp.int32)
    freq_bins = 1 + freq_ids * NT // (2 * FREQ)
    phase_ids = freq_bins[:, None] * sample_ids[None, :] % NT
    return phase_ids.astype(jnp.float32) * (2.0 * math.pi / NT)

def forward_table(sample_ids):
    angles = angle_table(sample_ids)
    return jnp.concatenate([jnp.cos(angles), -jnp.sin(angles)], 0) / math.sqrt(NT)

def inverse_table(sample_ids):
    angles = angle_table(sample_ids)
    return jnp.concatenate([jnp.cos(angles), -jnp.sin(angles)], 0) / math.sqrt(FREQ)

def trace_table(sample_ids):
    angles = angle_table(sample_ids)
    return jnp.concatenate([jnp.cos(angles), -jnp.sin(angles)], 0) * (2.0 / math.sqrt(NT))

def contract_last(left, right):
    return lax.dot_general(left, right, (((1,), (1,)), ((), ())), preferred_element_type=jnp.float32)

def contract_first(left, right):
    return lax.dot_general(left, right, (((0,), (0,)), ((), ())), preferred_element_type=jnp.float32)

def reference(f_time, reflect, band_map, gates):
    highest = lax.Precision.HIGHEST
    sample_ids = jnp.arange(NT, dtype=jnp.int32)
    forward_rows = forward_table(sample_ids)
    inverse_rows = inverse_table(sample_ids)
    trace_rows = trace_table(sample_ids)
    spectra = jnp.dot(forward_rows, f_time.reshape(NT, FOCAL * NR).astype(jnp.float32), precision=highest)
    spectra = spectra.reshape(2, FREQ, FOCAL, NR).astype(jnp.bfloat16)
    block_mask = jnp.repeat(jnp.repeat(band_map, SBLK, 0), RBLK, 1).astype(jnp.bfloat16)

    def forward_one(freq_id):
        real_resp = reflect[0, freq_id] * block_mask
        imag_resp = reflect[1, freq_id] * block_mask
        real_spec = spectra[0, freq_id]
        imag_spec = spectra[1, freq_id]
        real_part = contract_last(real_resp, real_spec) - contract_last(imag_resp, imag_spec)
        imag_part = contract_last(real_resp, imag_spec) + contract_last(imag_resp, real_spec)
        return jnp.stack([real_part, imag_part])
    forward = lax.map(forward_one, jnp.arange(FREQ, dtype=jnp.int32))
    forward = jnp.transpose(forward, (1, 0, 2, 3)).reshape(2 * FREQ, NS, FOCAL)
    gate_mask = (sample_ids[None, :] < gates[:, None]).astype(jnp.float32)
    weights = jnp.einsum('ot,pt,it->poi', forward_rows, gate_mask, trace_rows, precision=highest)
    windowed = jnp.einsum('poi,isp->osp', weights, forward, precision=highest)
    windowed = windowed.reshape(2, FREQ, NS, FOCAL).astype(jnp.bfloat16)

    def adjoint_one(freq_id):
        real_resp = reflect[0, freq_id] * block_mask
        imag_resp = reflect[1, freq_id] * block_mask
        real_gate = windowed[0, freq_id]
        imag_gate = windowed[1, freq_id]
        real_part = contract_first(real_resp, real_gate) + contract_first(imag_resp, imag_gate)
        imag_part = contract_first(real_resp, imag_gate) - contract_first(imag_resp, real_gate)
        return jnp.stack([real_part, imag_part])
    adjoint = lax.map(adjoint_one, jnp.arange(FREQ, dtype=jnp.int32))
    adjoint = jnp.transpose(adjoint, (1, 0, 2, 3)).reshape(2 * FREQ, NR, FOCAL)
    step_block = min(NT, 64)
    inverse_blocks = jnp.transpose(inverse_rows.reshape(2 * FREQ, NT // step_block, step_block), (1, 0, 2))

    def focus_block(rows_here):
        values = jnp.einsum('it,irp->tpr', rows_here, adjoint, precision=highest)
        return values.astype(jnp.bfloat16)
    focused = lax.map(focus_block, inverse_blocks)
    return focused.reshape(NT, FOCAL, NR)
```

```python
import math

import jax
import jax.numpy as jnp
from jax import lax
from jax.sharding import Mesh, PartitionSpec as P

NT = 512
FREQ = 8
HIGHEST = lax.Precision.HIGHEST
SRC = ("zh", "zl", "xl")
RCV = ("y", "xh")
PAIR = ("zl", "xl")


def angle_table(sample_ids):
    freq_ids = jnp.arange(FREQ, dtype=jnp.int32)
    freq_bins = 1 + freq_ids * NT // (2 * FREQ)
    phase_ids = freq_bins[:, None] * sample_ids[None, :] % NT
    return phase_ids.astype(jnp.float32) * (2.0 * math.pi / NT)


def wave_table(sample_ids, scale):
    angles = angle_table(sample_ids)
    rows = jnp.stack([jnp.cos(angles), -jnp.sin(angles)]) * scale
    rows = rows.reshape(2, 2, FREQ // 2, sample_ids.shape[0])
    return rows.transpose(1, 0, 2, 3).reshape(2 * FREQ, sample_ids.shape[0])


def shards(f_time, reflect, band_map, gates):
    local_steps, focal_here, rcv_here = f_time.shape
    freq_here, src_here = reflect.shape[1], reflect.shape[2]
    rows = 2 * freq_here
    zh, zl, xl = (lax.axis_size(a) for a in SRC)
    n_src = zh * zl * xl
    n_rcv = lax.axis_size(RCV)
    focal = n_src * focal_here
    frq_index = lax.axis_index("c")
    sample_ids = frq_index * local_steps + jnp.arange(local_steps, dtype=jnp.int32)

    partial_spec = jnp.dot(
        wave_table(sample_ids, 1.0 / math.sqrt(NT)),
        f_time.reshape(local_steps, focal_here * rcv_here).astype(jnp.float32),
        precision=HIGHEST,
    ).reshape(2, rows, focal_here, rcv_here)
    halves = lax.all_to_all(partial_spec, "c", 0, 0, tiled=True)
    spectra = (halves[0] + halves[1]).astype(jnp.bfloat16)
    near = lax.all_gather(spectra, "zh", axis=0)
    near = jnp.broadcast_to(near[None], (zl * xl,) + near.shape)
    every = lax.all_to_all(near, PAIR, 0, 0, tiled=True)
    spec = every.transpose(2, 0, 1, 3, 4).reshape(2, freq_here, focal, rcv_here)

    rows_block = src_here // band_map.shape[0]
    cols_block = rcv_here // band_map.shape[1]
    block_mask = jnp.repeat(jnp.repeat(band_map, rows_block, 0), cols_block, 1).astype(jnp.bfloat16)
    masked = reflect * block_mask[None, None]

    stacked_r = jnp.concatenate([spec[0], spec[1]], 1)
    stacked_i = jnp.concatenate([-spec[1], spec[0]], 1)
    forward = jnp.einsum("kqr,ksr->kqs", stacked_r, masked[0], preferred_element_type=jnp.float32)
    forward += jnp.einsum("kqr,ksr->kqs", stacked_i, masked[1], preferred_element_type=jnp.float32)
    focal_part = focal // (2 * n_rcv)
    parts = forward.reshape(freq_here, 2, 2 * n_rcv, focal_part, src_here)
    parts = parts.transpose(2, 3, 1, 0, 4).reshape(2 * n_rcv, focal_part, rows, src_here)
    parts = lax.all_to_all(parts, RCV + ("c",), 0, 0, tiled=True)
    summed = parts.reshape(n_rcv, 2, focal_part, rows, src_here).sum(0)

    mine = (lax.axis_index(RCV) * 2 + frq_index) * focal_part
    gate_order = gates.reshape(zh, zl * xl, focal_here).transpose(1, 0, 2).reshape(focal)
    own_gates = lax.dynamic_slice_in_dim(gate_order, mine, focal_part)
    all_samples = jnp.arange(NT, dtype=jnp.int32)
    gate_mask = (all_samples[None, :] < own_gates[:, None]).astype(jnp.float32)
    weights = jnp.einsum(
        "ot,pt,it->poi",
        wave_table(all_samples, 1.0 / math.sqrt(NT)),
        gate_mask,
        wave_table(all_samples, 2.0 / math.sqrt(NT)),
        precision=HIGHEST,
    )
    weights = weights.reshape(focal_part, 2, rows, 2, rows)
    gated = jnp.einsum("pgofi,fpis->gops", weights, summed, precision=HIGHEST).astype(jnp.bfloat16)
    gated = jnp.broadcast_to(gated[None], (n_rcv,) + gated.shape)
    gated = gated.reshape(2 * n_rcv, rows, focal_part, src_here)
    gated = lax.all_to_all(gated, RCV + ("c",), 0, 0, tiled=True)
    windowed = gated.transpose(1, 0, 2, 3).reshape(2, freq_here, focal, src_here)

    stacked_r = jnp.concatenate([windowed[0], windowed[1]], 1)
    stacked_i = jnp.concatenate([windowed[1], -windowed[0]], 1)
    adjoint = jnp.einsum("kqs,ksr->kqr", stacked_r, masked[0], preferred_element_type=jnp.float32)
    adjoint += jnp.einsum("kqs,ksr->kqr", stacked_i, masked[1], preferred_element_type=jnp.float32)
    sends = adjoint.astype(jnp.bfloat16).reshape(freq_here, 2, zl * xl, zh, focal_here, rcv_here)
    sends = sends.transpose(2, 3, 4, 1, 0, 5).reshape(zl * xl, zh, focal_here, rows, rcv_here)
    got = lax.all_to_all(sends, PAIR, 0, 0, tiled=True)
    got = got.astype(jnp.float32).sum(0)
    got = lax.all_to_all(got, "zh", 0, 0, tiled=True)
    own = got.sum(0)
    both = lax.all_gather(own, "c", axis=0)
    focused = jnp.einsum(
        "fit,fpir->tpr",
        wave_table(sample_ids, 1.0 / math.sqrt(FREQ)).reshape(2, rows, local_steps),
        both,
        precision=HIGHEST,
    )
    return focused.astype(jnp.bfloat16)


def solution(mesh):
    src, rcv, frq = (mesh.shape[a] for a in ("src", "rcv", "frq"))
    fine = Mesh(
        mesh.devices.reshape(src // 4, 2, 2, rcv // 2, 2, frq), SRC + RCV + ("c",)
    )
    return jax.shard_map(
        shards,
        mesh=fine,
        in_specs=(P("c", SRC, RCV), P(None, "c", SRC, RCV), P(SRC, RCV), P()),
        out_specs=P("c", SRC, RCV),
        check_vma=False,
    )
```

```python
import math

import jax
import jax.numpy as jnp
from jax import lax
from jax.experimental import pallas as pl
from jax.experimental.pallas import tpu as pltpu
from jax.sharding import Mesh, PartitionSpec as P

NT = 512
FREQ = 8
HALF = FREQ // 2
LANES = 128
HIGHEST = lax.Precision.HIGHEST
BF16 = jnp.bfloat16
F32 = jnp.float32
SRC = ("zh", "zl", "xl")
RCV = ("y", "xh")
PAIR = ("zl", "xl")
ROWS = 2 * HALF


def iota(shape, axis):
    return lax.broadcasted_iota(jnp.int32, shape, axis)


def wave(freq_ids, parts, sample_ids):
    phase = (1 + freq_ids * NT // (2 * FREQ)) * sample_ids % NT
    angle = phase.astype(F32) * (2.0 * math.pi / NT)
    return jnp.where(parts == 0, jnp.cos(angle), -jnp.sin(angle))


def thirds(x):
    high = lax.reduce_precision(x, 8, 7)
    middle = lax.reduce_precision(x - high, 8, 7)
    return high.astype(BF16), middle.astype(BF16), (x - high - middle).astype(BF16)


def vmem_call(body, out_shape, scratch=()):
    return pl.pallas_call(
        body,
        out_shape=out_shape,
        scratch_shapes=list(scratch),
        compiler_params=pltpu.CompilerParams(vmem_limit_bytes=32 << 20),
    )


def spectra_body(table_ref, f_ref, own_ref, other_ref):
    steps, focal, cols = f_ref.shape
    merged = f_ref[...].reshape(steps * focal, cols)
    sums = jnp.dot(table_ref[...], merged, preferred_element_type=F32)
    rows = sums.shape[0] // 3
    sums = sums[:rows] + sums[rows : 2 * rows] + sums[2 * rows :]
    own_ref[...] = sums[: rows // 2]
    other_ref[...] = sums[rows // 2 :]


def forward_body(spec_ref, resp_ref, out_ref, wide_ref, sums_ref):
    blocks = wide_ref.shape[0]
    points = spec_ref.shape[0] // ROWS
    chunks, _, lanes = out_ref.shape
    for j in range(blocks):
        wide_ref[j] = spec_ref[:, j * lanes : (j + 1) * lanes].astype(F32)

    def pick(row):
        pieces = [wide_ref[j, pl.ds(row, points, stride=ROWS), :] for j in range(blocks)]
        return jnp.concatenate(pieces, 1)

    for k in range(HALF):
        real, imag = pick(k), pick(HALF + k)
        first = jnp.concatenate([real, imag], 0).astype(BF16)
        second = jnp.concatenate([-imag, real], 0).astype(BF16)
        dims = (((1,), (1,)), ((), ()))
        sums = lax.dot_general(first, resp_ref[0, k], dims, preferred_element_type=F32)
        sums += lax.dot_general(second, resp_ref[1, k], dims, preferred_element_type=F32)
        head = sums[:, :lanes]
        rest = sums[:, lanes:]
        tail = jnp.concatenate(
            [rest, jnp.zeros((rest.shape[0], lanes - rest.shape[1]), F32)], 1
        )
        for part in range(2):
            at = pl.ds(part * HALF + k, points, stride=ROWS)
            sums_ref[0, at, :] = head[part * points : (part + 1) * points]
            sums_ref[1, at, :] = tail[part * points : (part + 1) * points]
    rows = points * ROWS // chunks
    for d in range(chunks):
        out_ref[d, :rows] = sums_ref[0, d * rows : (d + 1) * rows]
        tail = sums_ref[1, d * rows : (d + 1) * rows]
        out_ref[d, rows:] = tail[: rows // 2] + pltpu.roll(tail[rows // 2 :], lanes // 2, 1)


def gate_body(matrix_ref, parts_ref, out_ref):
    chunks, packed, lanes = parts_ref.shape
    rows = packed * 2 // 3
    cores = []
    for f in range(2):
        total = parts_ref[f]
        for d in range(f + 2, chunks, 2):
            total += parts_ref[d]
        tail = total[rows:]
        tail = jnp.concatenate([tail[:, : lanes // 2], tail[:, lanes // 2 :]], 0)
        cores.append(jnp.concatenate([total[:rows], tail], 1))
    gated = jnp.dot(
        matrix_ref[...], jnp.concatenate(cores, 0), precision=HIGHEST, preferred_element_type=F32
    ).astype(BF16)
    for f in range(2):
        mine = gated[f * rows : (f + 1) * rows]
        tail = mine[:, lanes:]
        tail = jnp.concatenate([tail[: rows // 2], tail[rows // 2 :]], 1)
        mine = jnp.concatenate([mine[:, :lanes], tail], 0)
        for d in range(f, chunks, 2):
            out_ref[d] = mine


def adjoint_body(win_ref, resp_ref, out_ref, wide_ref, sums_ref):
    chunks, packed, lanes = win_ref.shape
    rows = packed * 2 // 3
    points = chunks * rows // ROWS
    sources = resp_ref.shape[2]
    blocks = sums_ref.shape[0]
    for d in range(chunks):
        wide_ref[0, d * rows : (d + 1) * rows] = win_ref[d, :rows].astype(F32)
        tail = win_ref[d, rows:].astype(F32)
        half = d * rows + rows // 2
        wide_ref[1, d * rows : half] = tail
        wide_ref[1, half : (d + 1) * rows] = pltpu.roll(tail, lanes // 2, 1)

    def pick(row):
        pieces = [wide_ref[j, pl.ds(row, points, stride=ROWS), :] for j in range(2)]
        return jnp.concatenate(pieces, 1)[:, :sources]

    for k in range(HALF):
        real, imag = pick(k), pick(HALF + k)
        first = jnp.concatenate([real, imag], 0).astype(BF16)
        second = jnp.concatenate([imag, -real], 0).astype(BF16)
        sums = jnp.dot(first, resp_ref[0, k], preferred_element_type=F32)
        sums += jnp.dot(second, resp_ref[1, k], preferred_element_type=F32)
        for part in range(2):
            at = pl.ds(part * HALF + k, points, stride=ROWS)
            for j in range(blocks):
                sums_ref[j, at, :] = sums[
                    part * points : (part + 1) * points, j * lanes : (j + 1) * lanes
                ]
    for j in range(blocks):
        out_ref[:, j * lanes : (j + 1) * lanes] = sums_ref[j].astype(BF16)


def focused_body(table_ref, sums_ref, out_ref):
    steps, focal, cols = out_ref.shape
    x = sums_ref[...]
    high = x.astype(BF16)
    rest = x - high.astype(F32)
    middle = rest.astype(BF16)
    low = (rest - middle.astype(F32)).astype(BF16)
    right = jnp.concatenate([high, middle, high, low, high, middle], 0)
    values = jnp.dot(table_ref[...], right, preferred_element_type=F32)
    out_ref[...] = values.astype(BF16).reshape(steps, focal, cols)


def shards(f_time, reflect, band_map, gates):
    steps, focal_here, cols = f_time.shape
    sources = reflect.shape[2]
    zh, zl, xl = (lax.axis_size(a) for a in SRC)
    pairs = zl * xl
    n_rcv = lax.axis_size(RCV)
    chunks = 2 * n_rcv
    focal = zh * pairs * focal_here
    core = lax.axis_index("c")
    own_rows = focal_here * ROWS
    struct = jax.ShapeDtypeStruct

    shape = (2 * own_rows, steps * focal_here)
    row, col = iota(shape, 0), iota(shape, 1)
    held = jnp.where(row < own_rows, core, 1 - core)
    table = wave(held * HALF + row % HALF, row // HALF % 2, core * steps + col // focal_here)
    table = jnp.where(row // ROWS % focal_here == col % focal_here, table / math.sqrt(NT), 0.0)
    own, other = vmem_call(
        spectra_body, [struct((own_rows, cols), F32), struct((own_rows, cols), F32)]
    )(jnp.concatenate(thirds(table), 0), f_time)
    other = lax.ppermute(other, "c", [(0, 1), (1, 0)])
    spectra = (own + other).astype(BF16)
    near = jnp.broadcast_to(spectra[None], (zh, own_rows, cols))
    near = lax.all_to_all(near, "zh", 0, 0, tiled=True).reshape(zh * own_rows, cols)
    every = jnp.broadcast_to(near[None], (pairs, zh * own_rows, cols))
    every = lax.all_to_all(every, PAIR, 0, 0, tiled=True).reshape(focal * ROWS, cols)

    rows_block = sources // band_map.shape[0]
    cols_block = cols // band_map.shape[1]
    block_mask = jnp.repeat(jnp.repeat(band_map, rows_block, 0), cols_block, 1).astype(BF16)
    masked = reflect * block_mask[None, None]

    part_rows = focal * ROWS // chunks
    packed = part_rows * 3 // 2
    parts = vmem_call(
        forward_body,
        struct((chunks, packed, LANES), F32),
        [
            pltpu.VMEM((cols // LANES, focal * ROWS, LANES), F32),
            pltpu.VMEM((2, focal * ROWS, LANES), F32),
        ],
    )(every, masked)
    parts = lax.all_to_all(parts, RCV + ("c",), 0, 0, tiled=True)

    part_focal = part_rows // ROWS
    shape = (2 * part_rows, NT)
    row, col = iota(shape, 0), iota(shape, 1)
    waves = wave(row // part_rows * HALF + row % HALF, row // HALF % 2, col)
    point = (lax.axis_index(RCV) * 2 + core) * part_focal + iota((2 * part_rows, focal), 0) // ROWS % part_focal
    block = point // focal_here
    point = (block % zh * pairs + block // zh) * focal_here + point % focal_here
    window = jnp.where(point == iota((2 * part_rows, focal), 1), gates[None, :], 0).sum(1)
    inner = jnp.where(col < window[:, None], waves / math.sqrt(NT), 0.0)
    matrix = lax.dot_general(
        inner, waves * (2.0 / math.sqrt(NT)), (((1,), (1,)), ((), ())), precision=HIGHEST
    )
    shape = matrix.shape
    same = iota(shape, 0) // ROWS % part_focal == iota(shape, 1) // ROWS % part_focal
    matrix = jnp.where(same, matrix, 0.0)
    gated = vmem_call(gate_body, struct((chunks, packed, LANES), BF16))(matrix, parts)
    windowed = lax.all_to_all(gated, RCV + ("c",), 0, 0, tiled=True)

    sends = vmem_call(
        adjoint_body,
        struct((focal * ROWS, cols), BF16),
        [
            pltpu.VMEM((2, focal * ROWS, LANES), F32),
            pltpu.VMEM((cols // LANES, focal * ROWS, LANES), F32),
        ],
    )(windowed, masked)
    got = lax.all_to_all(sends.reshape(pairs, zh * own_rows, cols), PAIR, 0, 0, tiled=True)
    got = got.astype(F32).sum(0).astype(BF16).reshape(zh, own_rows, cols)
    got = lax.all_to_all(got, "zh", 0, 0, tiled=True)
    got = got.astype(F32).sum(0)
    both = lax.all_gather(got, "c", axis=0, tiled=True)

    shape = (steps * focal_here, 2 * own_rows)
    row, col = iota(shape, 0), iota(shape, 1)
    table = wave(col // own_rows * HALF + col % HALF, col // HALF % 2, core * steps + row // focal_here)
    table = jnp.where(col // ROWS % focal_here == row % focal_here, table / math.sqrt(FREQ), 0.0)
    high, middle, low = thirds(table)
    table = jnp.concatenate([high, high, middle, high, low, middle], 1)
    return vmem_call(focused_body, struct((steps, focal_here, cols), BF16))(table, both)


def solution(mesh):
    src, rcv, frq = (mesh.shape[a] for a in ("src", "rcv", "frq"))
    devices = mesh.devices.reshape(src // 4, 2, 2, rcv // 2, 2, frq)
    return jax.shard_map(
        shards,
        mesh=Mesh(devices, SRC + RCV + ("c",)),
        in_specs=(P("c", SRC, RCV), P(None, "c", SRC, RCV), P(SRC, RCV), P()),
        out_specs=P("c", SRC, RCV),
        check_vma=False,
    )
```

```python
import math

import jax
import jax.numpy as jnp
from jax import lax
from jax.experimental import pallas as pl
from jax.experimental.pallas import tpu as pltpu
from jax.sharding import Mesh, PartitionSpec as P

NT = 512
FREQ = 8
HALF = FREQ // 2
LANES = 128
HIGHEST = lax.Precision.HIGHEST
BF16 = jnp.bfloat16
F32 = jnp.float32
SRC = ("zh", "zl", "xl")
RCV = ("y", "xh")
PAIR = ("zl", "xl")
ROWS = 2 * HALF


def iota(shape, axis):
    return lax.broadcasted_iota(jnp.int32, shape, axis)


def wave(freq_ids, parts, sample_ids):
    phase = ((1 + freq_ids * NT // (2 * FREQ)) * sample_ids + parts * (NT // 4)) % NT
    return jnp.cos(phase.astype(F32) * (2.0 * math.pi / NT))


def thirds(x):
    high = lax.reduce_precision(x, 8, 7)
    middle = lax.reduce_precision(x - high, 8, 7)
    return high.astype(BF16), middle.astype(BF16), (x - high - middle).astype(BF16)


def vmem_call(body, out_shape, scratch=()):
    return pl.pallas_call(
        body,
        out_shape=out_shape,
        scratch_shapes=list(scratch),
        compiler_params=pltpu.CompilerParams(vmem_limit_bytes=12 << 20),
    )


def spectra_body(table_ref, f_ref, own_ref, other_ref):
    steps, focal, cols = f_ref.shape
    merged = f_ref[...].reshape(steps * focal, cols)
    sums = jnp.dot(table_ref[...], merged, preferred_element_type=F32)
    rows = sums.shape[0] // 3
    sums = sums[:rows] + sums[rows : 2 * rows] + sums[2 * rows :]
    own_ref[...] = sums[: rows // 2]
    other_ref[...] = sums[rows // 2 :]


def forward_body(spec_ref, resp_ref, out_ref, wide_ref, sums_ref):
    blocks = wide_ref.shape[0]
    points = spec_ref.shape[0] // ROWS
    chunks, _, lanes = out_ref.shape
    for j in range(blocks):
        wide_ref[j] = spec_ref[:, j * lanes : (j + 1) * lanes].astype(F32)

    def pick(row):
        pieces = [wide_ref[j, pl.ds(row, points, stride=ROWS), :] for j in range(blocks)]
        return jnp.concatenate(pieces, 1)

    for k in range(HALF):
        real, imag = pick(k), pick(HALF + k)
        first = jnp.concatenate([real, imag], 0).astype(BF16)
        second = jnp.concatenate([-imag, real], 0).astype(BF16)
        dims = (((1,), (1,)), ((), ()))
        sums = lax.dot_general(first, resp_ref[0, k], dims, preferred_element_type=F32)
        sums += lax.dot_general(second, resp_ref[1, k], dims, preferred_element_type=F32)
        head = sums[:, :lanes]
        rest = sums[:, lanes:]
        tail = jnp.concatenate(
            [rest, jnp.zeros((rest.shape[0], lanes - rest.shape[1]), F32)], 1
        )
        for part in range(2):
            at = pl.ds(part * HALF + k, points, stride=ROWS)
            sums_ref[0, at, :] = head[part * points : (part + 1) * points]
            sums_ref[1, at, :] = tail[part * points : (part + 1) * points]
    rows = points * ROWS // chunks
    for d in range(chunks):
        out_ref[d, :rows] = sums_ref[0, d * rows : (d + 1) * rows]
        tail = sums_ref[1, d * rows : (d + 1) * rows]
        out_ref[d, rows:] = tail[: rows // 2] + pltpu.roll(tail[rows // 2 :], lanes // 2, 1)


def gate_body(matrix_ref, parts_ref, out_ref):
    chunks, packed, lanes = parts_ref.shape
    rows = packed * 2 // 3
    cores = []
    for f in range(2):
        total = parts_ref[f]
        for d in range(f + 2, chunks, 2):
            total += parts_ref[d]
        tail = total[rows:]
        tail = jnp.concatenate([tail[:, : lanes // 2], tail[:, lanes // 2 :]], 0)
        cores.append(jnp.concatenate([total[:rows], tail], 1))
    gated = jnp.dot(
        matrix_ref[...], jnp.concatenate(cores, 0), precision=HIGHEST, preferred_element_type=F32
    ).astype(BF16)
    for f in range(2):
        mine = gated[f * rows : (f + 1) * rows]
        tail = mine[:, lanes:]
        tail = jnp.concatenate([tail[: rows // 2], tail[rows // 2 :]], 1)
        mine = jnp.concatenate([mine[:, :lanes], tail], 0)
        for d in range(f, chunks, 2):
            out_ref[d] = mine


def adjoint_body(win_ref, resp_ref, out_ref, wide_ref, sums_ref):
    chunks, packed, lanes = win_ref.shape
    rows = packed * 2 // 3
    points = chunks * rows // ROWS
    sources = resp_ref.shape[2]
    blocks = sums_ref.shape[0]
    for d in range(chunks):
        wide_ref[0, d * rows : (d + 1) * rows] = win_ref[d, :rows].astype(F32)
        tail = win_ref[d, rows:].astype(F32)
        half = d * rows + rows // 2
        wide_ref[1, d * rows : half] = tail
        wide_ref[1, half : (d + 1) * rows] = pltpu.roll(tail, lanes // 2, 1)

    def pick(row):
        pieces = [wide_ref[j, pl.ds(row, points, stride=ROWS), :] for j in range(2)]
        return jnp.concatenate(pieces, 1)[:, :sources]

    for k in range(HALF):
        real, imag = pick(k), pick(HALF + k)
        first = jnp.concatenate([real, imag], 0).astype(BF16)
        second = jnp.concatenate([imag, -real], 0).astype(BF16)
        sums = jnp.dot(first, resp_ref[0, k], preferred_element_type=F32)
        sums += jnp.dot(second, resp_ref[1, k], preferred_element_type=F32)
        for part in range(2):
            at = pl.ds(part * HALF + k, points, stride=ROWS)
            for j in range(blocks):
                sums_ref[j, at, :] = sums[
                    part * points : (part + 1) * points, j * lanes : (j + 1) * lanes
                ]
    for j in range(blocks):
        out_ref[:, j * lanes : (j + 1) * lanes] = sums_ref[j].astype(BF16)


def sum_body(got_ref, out_ref):
    total = got_ref[0].astype(F32)
    for d in range(1, got_ref.shape[0]):
        total += got_ref[d].astype(F32)
    out_ref[...] = total.astype(out_ref.dtype)


def focused_body(table_ref, sums_ref, out_ref):
    steps, focal, cols = out_ref.shape
    x = sums_ref[...]
    high = x.astype(BF16)
    rest = x - high.astype(F32)
    middle = rest.astype(BF16)
    low = (rest - middle.astype(F32)).astype(BF16)
    right = jnp.concatenate([high, middle, high, low, high, middle], 0)
    dims = (((0,), (0,)), ((), ()))
    values = lax.dot_general(table_ref[...], right, dims, preferred_element_type=F32)
    out_ref[...] = values.astype(BF16).reshape(steps, focal, cols)


def focal_table(core_ids, core, steps, focal, scale):
    shape = (2 * focal * ROWS, steps * focal)
    row, col = iota(shape, 0), iota(shape, 1)
    held = jnp.where(row < focal * ROWS, core_ids[0], core_ids[1])
    table = wave(held * HALF + row % HALF, row // HALF % 2, core * steps + col // focal)
    return thirds(jnp.where(row // ROWS % focal == col % focal, table * scale, 0.0))


def shards(f_time, reflect, band_map, gates):
    steps, focal_here, cols = f_time.shape
    sources = reflect.shape[2]
    zh, zl, xl = (lax.axis_size(a) for a in SRC)
    pairs = zl * xl
    n_rcv = lax.axis_size(RCV)
    chunks = 2 * n_rcv
    focal = zh * pairs * focal_here
    core = lax.axis_index("c")
    own_rows = focal_here * ROWS
    struct = jax.ShapeDtypeStruct

    table = focal_table((core, 1 - core), core, steps, focal_here, 1.0 / math.sqrt(NT))
    own, other = vmem_call(
        spectra_body, [struct((own_rows, cols), F32), struct((own_rows, cols), F32)]
    )(jnp.concatenate(table, 0), f_time)
    other = lax.ppermute(other, "c", [(0, 1), (1, 0)])
    spectra = (own + other).astype(BF16)
    near = jnp.broadcast_to(spectra[None], (zh, own_rows, cols))
    near = lax.all_to_all(near, "zh", 0, 0, tiled=True).reshape(zh * own_rows, cols)
    every = jnp.broadcast_to(near[None], (pairs, zh * own_rows, cols))
    every = lax.all_to_all(every, PAIR, 0, 0, tiled=True).reshape(focal * ROWS, cols)

    rows_block = sources // band_map.shape[0]
    cols_block = cols // band_map.shape[1]
    block_mask = jnp.repeat(jnp.repeat(band_map, rows_block, 0), cols_block, 1).astype(BF16)
    masked = reflect * block_mask[None, None]

    part_rows = focal * ROWS // chunks
    part_focal = part_rows // ROWS
    shape = (2 * part_rows, NT)
    row, col = iota(shape, 0), iota(shape, 1)
    waves = wave(row // part_rows * HALF + row % HALF, row // HALF % 2, col)
    point = (lax.axis_index(RCV) * 2 + core) * part_focal + iota((2 * part_rows, focal), 0) // ROWS % part_focal
    block = point // focal_here
    point = (block % zh * pairs + block // zh) * focal_here + point % focal_here
    window = jnp.where(point == iota((2 * part_rows, focal), 1), gates[None, :], 0).sum(1)
    inner = jnp.where(col < window[:, None], waves / math.sqrt(NT), 0.0)
    matrix = lax.dot_general(
        inner, waves * (2.0 / math.sqrt(NT)), (((1,), (1,)), ((), ())), precision=HIGHEST
    )
    shape = matrix.shape
    same = iota(shape, 0) // ROWS % part_focal == iota(shape, 1) // ROWS % part_focal
    matrix = jnp.where(same, matrix, 0.0)
    high, middle, low = focal_table((0, 1), core, steps, focal_here, 1.0 / math.sqrt(FREQ))
    table = jnp.concatenate([high, high, middle, high, low, middle], 0)
    every, masked, matrix, table = lax.optimization_barrier((every, masked, matrix, table))

    packed = part_rows * 3 // 2
    parts = vmem_call(
        forward_body,
        struct((chunks, packed, LANES), F32),
        [
            pltpu.VMEM((cols // LANES, focal * ROWS, LANES), F32),
            pltpu.VMEM((2, focal * ROWS, LANES), F32),
        ],
    )(every, masked)
    parts = lax.all_to_all(parts, RCV + ("c",), 0, 0, tiled=True)

    gated = vmem_call(gate_body, struct((chunks, packed, LANES), BF16))(matrix, parts)
    windowed = lax.all_to_all(gated, RCV + ("c",), 0, 0, tiled=True)

    sends = vmem_call(
        adjoint_body,
        struct((focal * ROWS, cols), BF16),
        [
            pltpu.VMEM((2, focal * ROWS, LANES), F32),
            pltpu.VMEM((cols // LANES, focal * ROWS, LANES), F32),
        ],
    )(windowed, masked)
    got = lax.all_to_all(sends.reshape(pairs, zh * own_rows, cols), PAIR, 0, 0, tiled=True)
    got = vmem_call(sum_body, struct((zh * own_rows, cols), BF16))(got)
    got = lax.all_to_all(got.reshape(zh, own_rows, cols), "zh", 0, 0, tiled=True)
    got = vmem_call(sum_body, struct((own_rows, cols), F32))(got)
    both = lax.all_gather(got, "c", axis=0, tiled=True)

    block = steps // 4
    return pl.pallas_call(
        focused_body,
        out_shape=struct((steps, focal_here, cols), BF16),
        grid=(4,),
        in_specs=[
            pl.BlockSpec((table.shape[0], block * focal_here), lambda i: (0, i)),
            pl.BlockSpec((2 * own_rows, cols), lambda i: (0, 0)),
        ],
        out_specs=pl.BlockSpec((block, focal_here, cols), lambda i: (i, 0, 0)),
        compiler_params=pltpu.CompilerParams(vmem_limit_bytes=12 << 20),
    )(table, both)


def solution(mesh):
    src, rcv, frq = (mesh.shape[a] for a in ("src", "rcv", "frq"))
    devices = mesh.devices.reshape(src // 4, 2, 2, rcv // 2, 2, frq)
    return jax.shard_map(
        shards,
        mesh=Mesh(devices, SRC + RCV + ("c",)),
        in_specs=(P("c", SRC, RCV), P(None, "c", SRC, RCV), P(SRC, RCV), P()),
        out_specs=P("c", SRC, RCV),
        check_vma=False,
    )
```

```python
import math

import jax
import jax.numpy as jnp
from jax import lax
from jax.experimental import pallas as pl
from jax.experimental.pallas import tpu as pltpu
from jax.sharding import Mesh, PartitionSpec as P

NT = 512
FREQ = 8
HALF = FREQ // 2
LANES = 128
HIGHEST = lax.Precision.HIGHEST
BF16 = jnp.bfloat16
F32 = jnp.float32
SRC = ("zh", "zl", "xl")
RCV = ("y", "xh")
PAIR = ("zl", "xl")
ROWS = 2 * HALF


def iota(shape, axis):
    return lax.broadcasted_iota(jnp.int32, shape, axis)


def wave(freq_ids, parts, sample_ids):
    phase = ((1 + freq_ids * NT // (2 * FREQ)) * sample_ids + parts * (NT // 4)) % NT
    return jnp.cos(phase.astype(F32) * (2.0 * math.pi / NT))


def thirds(x):
    high = x.astype(BF16)
    rest = x - high.astype(F32)
    middle = rest.astype(BF16)
    return high, middle, (rest - middle.astype(F32)).astype(BF16)


def vmem_call(body, out_shape, scratch=()):
    return pl.pallas_call(
        body,
        out_shape=out_shape,
        scratch_shapes=list(scratch),
        compiler_params=pltpu.CompilerParams(vmem_limit_bytes=12 << 20),
    )


def spectra_body(f_ref, own_ref, other_ref, last_ref, held_ref, sem_ref):
    copy = pltpu.make_async_copy(f_ref, held_ref, sem_ref)
    copy.start()
    steps, focal, cols = f_ref.shape
    core = lax.axis_index("c")
    table = focal_table((core, 1 - core), core, steps, focal, 1.0 / math.sqrt(NT))
    rows = table.shape[0]
    table = jnp.concatenate(thirds(table), 0)
    high, middle, low = thirds(focal_table((0, 1), core, steps, focal, 1.0 / math.sqrt(FREQ)))
    last_ref[...] = jnp.concatenate([high, high, middle, high, low, middle], 0)
    copy.wait()
    merged = held_ref[...].reshape(steps * focal, cols)
    sums = jnp.dot(table, merged, preferred_element_type=F32)
    sums = sums[:rows] + sums[rows : 2 * rows] + sums[2 * rows :]
    own_ref[...] = sums[: rows // 2]
    other_ref[...] = sums[rows // 2 :]


def forward_body(spec_ref, resp_ref, out_ref, wide_ref, sums_ref):
    blocks = wide_ref.shape[0]
    points = spec_ref.shape[0] // ROWS
    chunks, _, lanes = out_ref.shape
    for j in range(blocks):
        wide_ref[j] = spec_ref[:, j * lanes : (j + 1) * lanes].astype(F32)

    def pick(row):
        pieces = [wide_ref[j, pl.ds(row, points, stride=ROWS), :] for j in range(blocks)]
        return jnp.concatenate(pieces, 1)

    for k in range(HALF):
        real, imag = pick(k), pick(HALF + k)
        first = jnp.concatenate([real, imag], 0).astype(BF16)
        second = jnp.concatenate([-imag, real], 0).astype(BF16)
        dims = (((1,), (1,)), ((), ()))
        sums = lax.dot_general(first, resp_ref[0, k], dims, preferred_element_type=F32)
        sums += lax.dot_general(second, resp_ref[1, k], dims, preferred_element_type=F32)
        head = sums[:, :lanes]
        rest = sums[:, lanes:]
        tail = jnp.concatenate(
            [rest, jnp.zeros((rest.shape[0], lanes - rest.shape[1]), F32)], 1
        )
        for part in range(2):
            at = pl.ds(part * HALF + k, points, stride=ROWS)
            sums_ref[0, at, :] = head[part * points : (part + 1) * points]
            sums_ref[1, at, :] = tail[part * points : (part + 1) * points]
    rows = points * ROWS // chunks
    for d in range(chunks):
        out_ref[d, :rows] = sums_ref[0, d * rows : (d + 1) * rows]
        tail = sums_ref[1, d * rows : (d + 1) * rows]
        out_ref[d, rows:] = tail[: rows // 2] + pltpu.roll(tail[rows // 2 :], lanes // 2, 1)


def gate_body(matrix_ref, parts_ref, out_ref):
    chunks, packed, lanes = parts_ref.shape
    rows = packed * 2 // 3
    cores = []
    for f in range(2):
        total = parts_ref[f]
        for d in range(f + 2, chunks, 2):
            total += parts_ref[d]
        tail = total[rows:]
        tail = jnp.concatenate([tail[:, : lanes // 2], tail[:, lanes // 2 :]], 0)
        cores.append(jnp.concatenate([total[:rows], tail], 1))
    gated = jnp.dot(
        matrix_ref[...], jnp.concatenate(cores, 0), precision=HIGHEST, preferred_element_type=F32
    ).astype(BF16)
    for f in range(2):
        mine = gated[f * rows : (f + 1) * rows]
        tail = mine[:, lanes:]
        tail = jnp.concatenate([tail[: rows // 2], tail[rows // 2 :]], 1)
        mine = jnp.concatenate([mine[:, :lanes], tail], 0)
        for d in range(f, chunks, 2):
            out_ref[d] = mine


def adjoint_body(win_ref, resp_ref, out_ref, wide_ref, sums_ref):
    chunks, packed, lanes = win_ref.shape
    rows = packed * 2 // 3
    points = chunks * rows // ROWS
    sources = resp_ref.shape[2]
    blocks = sums_ref.shape[0]
    for d in range(chunks):
        wide_ref[0, d * rows : (d + 1) * rows] = win_ref[d, :rows].astype(F32)
        tail = win_ref[d, rows:].astype(F32)
        half = d * rows + rows // 2
        wide_ref[1, d * rows : half] = tail
        wide_ref[1, half : (d + 1) * rows] = pltpu.roll(tail, lanes // 2, 1)

    def pick(row):
        pieces = [wide_ref[j, pl.ds(row, points, stride=ROWS), :] for j in range(2)]
        return jnp.concatenate(pieces, 1)[:, :sources]

    for k in range(HALF):
        real, imag = pick(k), pick(HALF + k)
        first = jnp.concatenate([real, imag], 0).astype(BF16)
        second = jnp.concatenate([imag, -real], 0).astype(BF16)
        sums = jnp.dot(first, resp_ref[0, k], preferred_element_type=F32)
        sums += jnp.dot(second, resp_ref[1, k], preferred_element_type=F32)
        for part in range(2):
            at = pl.ds(part * HALF + k, points, stride=ROWS)
            for j in range(blocks):
                sums_ref[j, at, :] = sums[
                    part * points : (part + 1) * points, j * lanes : (j + 1) * lanes
                ]
    for j in range(blocks):
        out_ref[:, j * lanes : (j + 1) * lanes] = sums_ref[j].astype(BF16)


def sum_body(got_ref, out_ref):
    total = got_ref[0].astype(F32)
    for d in range(1, got_ref.shape[0]):
        total += got_ref[d].astype(F32)
    out_ref[...] = total.astype(out_ref.dtype)


def focused_body(table_ref, sums_ref, out_ref, held_ref, sem_ref):
    steps, focal, cols = out_ref.shape
    high, middle, low = thirds(sums_ref[...])
    right = jnp.concatenate([high, middle, high, low, high, middle], 0)
    dims = (((0,), (0,)), ((), ()))
    pieces = sem_ref.shape[0]
    block = steps // pieces
    copies = []
    for i in range(pieces):
        left = table_ref[:, i * block * focal : (i + 1) * block * focal]
        values = lax.dot_general(left, right, dims, preferred_element_type=F32)
        at = pl.ds(i * block, block)
        held_ref[at] = values.astype(BF16).reshape(block, focal, cols)
        copies.append(pltpu.make_async_copy(held_ref.at[at], out_ref.at[at], sem_ref.at[i]))
        copies[-1].start()
    for copy in copies:
        copy.wait()


def focal_table(core_ids, core, steps, focal, scale):
    shape = (2 * focal * ROWS, steps * focal)
    row, col = iota(shape, 0), iota(shape, 1)
    held = jnp.where(row < focal * ROWS, core_ids[0], core_ids[1])
    table = wave(held * HALF + row % HALF, row // HALF % 2, core * steps + col // focal)
    return jnp.where(row // ROWS % focal == col % focal, table * scale, 0.0)


def shards(f_time, reflect, band_map, gates):
    steps, focal_here, cols = f_time.shape
    sources = reflect.shape[2]
    zh, zl, xl = (lax.axis_size(a) for a in SRC)
    pairs = zl * xl
    n_rcv = lax.axis_size(RCV)
    chunks = 2 * n_rcv
    focal = zh * pairs * focal_here
    core = lax.axis_index("c")
    own_rows = focal_here * ROWS
    struct = jax.ShapeDtypeStruct

    own, other, table = pl.pallas_call(
        spectra_body,
        out_shape=[struct((own_rows, cols), F32)] * 2
        + [struct((6 * 2 * own_rows, steps * focal_here), BF16)],
        in_specs=[pl.BlockSpec(memory_space=pltpu.HBM)],
        scratch_shapes=[pltpu.VMEM(f_time.shape, BF16), pltpu.SemaphoreType.DMA],
        compiler_params=pltpu.CompilerParams(vmem_limit_bytes=54784 << 10),
    )(f_time)
    other = lax.ppermute(other, "c", [(0, 1), (1, 0)])
    other, core, gates, band_map = lax.optimization_barrier((other, core, gates, band_map))
    spectra = (own + other).astype(BF16)
    near = jnp.broadcast_to(spectra[None], (zh, own_rows, cols))
    near = lax.all_to_all(near, "zh", 0, 0, tiled=True).reshape(zh * own_rows, cols)

    rows_block = sources // band_map.shape[0]
    cols_block = cols // band_map.shape[1]
    block_mask = jnp.repeat(jnp.repeat(band_map, rows_block, 0), cols_block, 1).astype(BF16)
    masked = reflect * block_mask[None, None]

    part_rows = focal * ROWS // chunks
    part_focal = part_rows // ROWS
    shape = (2 * part_rows, NT)
    row, col = iota(shape, 0), iota(shape, 1)
    waves = wave(row // part_rows * HALF + row % HALF, row // HALF % 2, col)
    point = (lax.axis_index(RCV) * 2 + core) * part_focal + iota((2 * part_rows, focal), 0) // ROWS % part_focal
    block = point // focal_here
    point = (block % zh * pairs + block // zh) * focal_here + point % focal_here
    window = jnp.where(point == iota((2 * part_rows, focal), 1), gates[None, :], 0).sum(1)
    inner = jnp.where(col < window[:, None], waves / math.sqrt(NT), 0.0)
    matrix = lax.dot_general(
        inner, waves * (2.0 / math.sqrt(NT)), (((1,), (1,)), ((), ())), precision=HIGHEST
    )
    shape = matrix.shape
    same = iota(shape, 0) // ROWS % part_focal == iota(shape, 1) // ROWS % part_focal
    matrix = jnp.where(same, matrix, 0.0)
    near, masked, matrix = lax.optimization_barrier((near, masked, matrix))
    every = jnp.broadcast_to(near[None], (pairs, zh * own_rows, cols))
    every = lax.all_to_all(every, PAIR, 0, 0, tiled=True).reshape(focal * ROWS, cols)

    packed = part_rows * 3 // 2
    parts = vmem_call(
        forward_body,
        struct((chunks, packed, LANES), F32),
        [
            pltpu.VMEM((cols // LANES, focal * ROWS, LANES), F32),
            pltpu.VMEM((2, focal * ROWS, LANES), F32),
        ],
    )(every, masked)
    parts = lax.all_to_all(parts, RCV + ("c",), 0, 0, tiled=True)

    gated = vmem_call(gate_body, struct((chunks, packed, LANES), BF16))(matrix, parts)
    windowed = lax.all_to_all(gated, RCV + ("c",), 0, 0, tiled=True)

    sends = vmem_call(
        adjoint_body,
        struct((focal * ROWS, cols), BF16),
        [
            pltpu.VMEM((2, focal * ROWS, LANES), F32),
            pltpu.VMEM((cols // LANES, focal * ROWS, LANES), F32),
        ],
    )(windowed, masked)
    got = lax.all_to_all(sends.reshape(pairs, zh * own_rows, cols), PAIR, 0, 0, tiled=True)
    got = vmem_call(sum_body, struct((zh * own_rows, cols), BF16))(got)
    got = lax.all_to_all(got.reshape(zh, own_rows, cols), "zh", 0, 0, tiled=True)
    got = vmem_call(sum_body, struct((own_rows, cols), F32))(got)
    both = lax.all_gather(got, "c", axis=0, tiled=True)

    return pl.pallas_call(
        focused_body,
        out_shape=struct((steps, focal_here, cols), BF16),
        in_specs=[pl.BlockSpec(memory_space=pltpu.VMEM)] * 2,
        out_specs=pl.BlockSpec(memory_space=pltpu.HBM),
        scratch_shapes=[pltpu.VMEM(f_time.shape, BF16), pltpu.SemaphoreType.DMA((2,))],
        compiler_params=pltpu.CompilerParams(vmem_limit_bytes=12 << 20),
    )(table, both)


def solution(mesh):
    src, rcv, frq = (mesh.shape[a] for a in ("src", "rcv", "frq"))
    devices = mesh.devices.reshape(src // 4, 2, 2, rcv // 2, 2, frq)
    return jax.shard_map(
        shards,
        mesh=Mesh(devices, SRC + RCV + ("c",)),
        in_specs=(P("c", SRC, RCV), P(None, "c", SRC, RCV), P(SRC, RCV), P()),
        out_specs=P("c", SRC, RCV),
        check_vma=False,
    )
```

```python
import math

import jax
import jax.numpy as jnp
from jax import lax
from jax.experimental import pallas as pl
from jax.experimental.pallas import tpu as pltpu
from jax.sharding import Mesh, PartitionSpec as P

NT = 512
FREQ = 8
HALF = FREQ // 2
LANES = 128
HIGHEST = lax.Precision.HIGHEST
BF16 = jnp.bfloat16
F32 = jnp.float32
SRC = ("zh", "zl", "xl")
RCV = ("y", "xh")
PAIR = ("zl", "xl")
ROWS = 2 * HALF


def iota(shape, axis):
    return lax.broadcasted_iota(jnp.int32, shape, axis)


def wave(freq_ids, parts, sample_ids):
    phase = ((1 + freq_ids * NT // (2 * FREQ)) * sample_ids + parts * (NT // 4)) % NT
    return jnp.cos(phase.astype(F32) * (2.0 * math.pi / NT))


def thirds(x):
    high = x.astype(BF16)
    rest = x - high.astype(F32)
    middle = rest.astype(BF16)
    return high, middle, (rest - middle.astype(F32)).astype(BF16)


def vmem_call(body, out_shape, scratch=(), cost=None):
    return pl.pallas_call(
        body,
        out_shape=out_shape,
        scratch_shapes=list(scratch),
        cost_estimate=cost,
        compiler_params=pltpu.CompilerParams(vmem_limit_bytes=12 << 20),
    )


def spectra_body(f_ref, own_ref, other_ref, last_ref, held_ref, sem_ref):
    copy = pltpu.make_async_copy(f_ref, held_ref, sem_ref)
    copy.start()
    steps, focal, cols = f_ref.shape
    core = lax.axis_index("c")
    table = focal_table((core, 1 - core), core, steps, focal, 1.0 / math.sqrt(NT))
    rows = table.shape[0]
    table = jnp.concatenate(thirds(table), 0)
    high, middle, low = thirds(focal_table((0, 1), core, steps, focal, 1.0 / math.sqrt(FREQ)))
    last_ref[...] = jnp.concatenate([high, high, middle, high, low, middle], 0)
    copy.wait()
    merged = held_ref[...].reshape(steps * focal, cols)
    sums = jnp.dot(table, merged, preferred_element_type=F32)
    sums = sums[:rows] + sums[rows : 2 * rows] + sums[2 * rows :]
    own_ref[...] = sums[: rows // 2]
    other_ref[...] = sums[rows // 2 :]


def masked_body(band_ref, resp_ref, out_ref):
    band = band_ref[...].astype(F32).astype(BF16)
    down, across = band.shape
    parts, _, sources, cols = resp_ref.shape
    shape = (across, cols)
    picks = (iota(shape, 0) == iota(shape, 1) // (cols // across)).astype(F32).astype(BF16)
    wide = jnp.dot(band, picks, preferred_element_type=F32).astype(BF16)
    shape = (sources, down)
    picks = (iota(shape, 0) // (sources // down) == iota(shape, 1)).astype(F32).astype(BF16)
    mask = jnp.dot(picks, wide, preferred_element_type=F32).astype(BF16)
    for c in range(parts):
        for k in range(HALF):
            out_ref[c, k] = resp_ref[c, k] * mask


def forward_body(spec_ref, resp_ref, out_ref, wide_ref, sums_ref):
    blocks = wide_ref.shape[0]
    points = spec_ref.shape[0] // ROWS
    chunks, _, lanes = out_ref.shape
    for j in range(blocks):
        wide_ref[j] = spec_ref[:, j * lanes : (j + 1) * lanes].astype(F32)

    def pick(row):
        pieces = [wide_ref[j, pl.ds(row, points, stride=ROWS), :] for j in range(blocks)]
        return jnp.concatenate(pieces, 1)

    for k in range(HALF):
        real, imag = pick(k), pick(HALF + k)
        first = jnp.concatenate([real, imag], 0).astype(BF16)
        second = jnp.concatenate([-imag, real], 0).astype(BF16)
        dims = (((1,), (1,)), ((), ()))
        sums = lax.dot_general(first, resp_ref[0, k], dims, preferred_element_type=F32)
        sums += lax.dot_general(second, resp_ref[1, k], dims, preferred_element_type=F32)
        head = sums[:, :lanes]
        rest = sums[:, lanes:]
        tail = jnp.concatenate(
            [rest, jnp.zeros((rest.shape[0], lanes - rest.shape[1]), F32)], 1
        )
        for part in range(2):
            at = pl.ds(part * HALF + k, points, stride=ROWS)
            sums_ref[0, at, :] = head[part * points : (part + 1) * points]
            sums_ref[1, at, :] = tail[part * points : (part + 1) * points]
    rows = points * ROWS // chunks
    for d in range(chunks):
        out_ref[d, :rows] = sums_ref[0, d * rows : (d + 1) * rows]
        tail = sums_ref[1, d * rows : (d + 1) * rows]
        out_ref[d, rows:] = tail[: rows // 2] + pltpu.roll(tail[rows // 2 :], lanes // 2, 1)


def gate_body(matrix_ref, parts_ref, out_ref):
    chunks, packed, lanes = parts_ref.shape
    rows = packed * 2 // 3
    cores = []
    for f in range(2):
        total = parts_ref[f]
        for d in range(f + 2, chunks, 2):
            total += parts_ref[d]
        tail = total[rows:]
        tail = jnp.concatenate([tail[:, : lanes // 2], tail[:, lanes // 2 :]], 0)
        cores.append(jnp.concatenate([total[:rows], tail], 1))
    gated = jnp.dot(
        matrix_ref[...], jnp.concatenate(cores, 0), precision=HIGHEST, preferred_element_type=F32
    ).astype(BF16)
    for f in range(2):
        mine = gated[f * rows : (f + 1) * rows]
        tail = mine[:, lanes:]
        tail = jnp.concatenate([tail[: rows // 2], tail[rows // 2 :]], 1)
        mine = jnp.concatenate([mine[:, :lanes], tail], 0)
        for d in range(f, chunks, 2):
            out_ref[d] = mine


def adjoint_body(win_ref, resp_ref, out_ref, wide_ref, sums_ref):
    chunks, packed, lanes = win_ref.shape
    rows = packed * 2 // 3
    points = chunks * rows // ROWS
    sources = resp_ref.shape[2]
    blocks = sums_ref.shape[0]
    for d in range(chunks):
        wide_ref[0, d * rows : (d + 1) * rows] = win_ref[d, :rows].astype(F32)
        tail = win_ref[d, rows:].astype(F32)
        half = d * rows + rows // 2
        wide_ref[1, d * rows : half] = tail
        wide_ref[1, half : (d + 1) * rows] = pltpu.roll(tail, lanes // 2, 1)

    def pick(row):
        pieces = [wide_ref[j, pl.ds(row, points, stride=ROWS), :] for j in range(2)]
        return jnp.concatenate(pieces, 1)[:, :sources]

    for k in range(HALF):
        real, imag = pick(k), pick(HALF + k)
        first = jnp.concatenate([real, imag], 0).astype(BF16)
        second = jnp.concatenate([imag, -real], 0).astype(BF16)
        sums = jnp.dot(first, resp_ref[0, k], preferred_element_type=F32)
        sums += jnp.dot(second, resp_ref[1, k], preferred_element_type=F32)
        for part in range(2):
            at = pl.ds(part * HALF + k, points, stride=ROWS)
            for j in range(blocks):
                sums_ref[j, at, :] = sums[
                    part * points : (part + 1) * points, j * lanes : (j + 1) * lanes
                ]
    for j in range(blocks):
        out_ref[:, j * lanes : (j + 1) * lanes] = sums_ref[j].astype(BF16)


def sum_body(got_ref, out_ref):
    total = got_ref[0].astype(F32)
    for d in range(1, got_ref.shape[0]):
        total += got_ref[d].astype(F32)
    out_ref[...] = total.astype(out_ref.dtype)


def focused_body(table_ref, sums_ref, out_ref, held_ref, sem_ref):
    steps, focal, cols = out_ref.shape
    high, middle, low = thirds(sums_ref[...])
    right = jnp.concatenate([high, middle, high, low, high, middle], 0)
    dims = (((0,), (0,)), ((), ()))
    pieces = sem_ref.shape[0]
    block = steps // pieces
    copies = []
    for i in range(pieces):
        left = table_ref[:, i * block * focal : (i + 1) * block * focal]
        values = lax.dot_general(left, right, dims, preferred_element_type=F32)
        at = pl.ds(i * block, block)
        held_ref[at] = values.astype(BF16).reshape(block, focal, cols)
        copies.append(pltpu.make_async_copy(held_ref.at[at], out_ref.at[at], sem_ref.at[i]))
        copies[-1].start()
    for copy in copies:
        copy.wait()


def focal_table(core_ids, core, steps, focal, scale):
    shape = (2 * focal * ROWS, steps * focal)
    row, col = iota(shape, 0), iota(shape, 1)
    held = jnp.where(row < focal * ROWS, core_ids[0], core_ids[1])
    table = wave(held * HALF + row % HALF, row // HALF % 2, core * steps + col // focal)
    return jnp.where(row // ROWS % focal == col % focal, table * scale, 0.0)


def shards(f_time, reflect, band_map, gates):
    steps, focal_here, cols = f_time.shape
    sources = reflect.shape[2]
    zh, zl, xl = (lax.axis_size(a) for a in SRC)
    pairs = zl * xl
    n_rcv = lax.axis_size(RCV)
    chunks = 2 * n_rcv
    focal = zh * pairs * focal_here
    core = lax.axis_index("c")
    own_rows = focal_here * ROWS
    struct = jax.ShapeDtypeStruct

    own, other, table = pl.pallas_call(
        spectra_body,
        out_shape=[struct((own_rows, cols), F32)] * 2
        + [struct((6 * 2 * own_rows, steps * focal_here), BF16)],
        in_specs=[pl.BlockSpec(memory_space=pltpu.HBM)],
        scratch_shapes=[pltpu.VMEM(f_time.shape, BF16), pltpu.SemaphoreType.DMA],
        compiler_params=pltpu.CompilerParams(vmem_limit_bytes=54784 << 10),
    )(f_time)
    others = lax.all_gather(other, "c", axis=0)
    others, core, gates, band_map = lax.optimization_barrier((others, core, gates, band_map))
    other = jnp.where(core == 0, others[1], others[0])
    spectra = (own + other).astype(BF16)
    near = jnp.broadcast_to(spectra[None], (zh, own_rows, cols))
    near = lax.all_to_all(near, "zh", 0, 0, tiled=True).reshape(zh * own_rows, cols)

    masked = vmem_call(
        masked_body,
        struct(reflect.shape, BF16),
        cost=pl.CostEstimate(flops=reflect.size, transcendentals=0, bytes_accessed=4 * reflect.size),
    )(band_map, reflect)

    part_rows = focal * ROWS // chunks
    part_focal = part_rows // ROWS
    shape = (2 * part_rows, NT)
    row, col = iota(shape, 0), iota(shape, 1)
    waves = wave(row // part_rows * HALF + row % HALF, row // HALF % 2, col)
    point = (lax.axis_index(RCV) * 2 + core) * part_focal + iota((2 * part_rows, focal), 0) // ROWS % part_focal
    block = point // focal_here
    point = (block % zh * pairs + block // zh) * focal_here + point % focal_here
    window = jnp.where(point == iota((2 * part_rows, focal), 1), gates[None, :], 0).sum(1)
    inner = jnp.where(col < window[:, None], waves / math.sqrt(NT), 0.0)
    matrix = lax.dot_general(
        inner, waves * (2.0 / math.sqrt(NT)), (((1,), (1,)), ((), ())), precision=HIGHEST
    )
    shape = matrix.shape
    same = iota(shape, 0) // ROWS % part_focal == iota(shape, 1) // ROWS % part_focal
    matrix = jnp.where(same, matrix, 0.0)
    near, masked, matrix = lax.optimization_barrier((near, masked, matrix))
    every = jnp.broadcast_to(near[None], (pairs, zh * own_rows, cols))
    every = lax.all_to_all(every, PAIR, 0, 0, tiled=True).reshape(focal * ROWS, cols)

    packed = part_rows * 3 // 2
    parts = vmem_call(
        forward_body,
        struct((chunks, packed, LANES), F32),
        [
            pltpu.VMEM((cols // LANES, focal * ROWS, LANES), F32),
            pltpu.VMEM((2, focal * ROWS, LANES), F32),
        ],
    )(every, masked)
    parts = lax.all_to_all(parts, RCV + ("c",), 0, 0, tiled=True)

    gated = vmem_call(gate_body, struct((chunks, packed, LANES), BF16))(matrix, parts)
    windowed = lax.all_to_all(gated, RCV + ("c",), 0, 0, tiled=True)

    sends = vmem_call(
        adjoint_body,
        struct((focal * ROWS, cols), BF16),
        [
            pltpu.VMEM((2, focal * ROWS, LANES), F32),
            pltpu.VMEM((cols // LANES, focal * ROWS, LANES), F32),
        ],
    )(windowed, masked)
    got = lax.all_to_all(sends.reshape(pairs, zh * own_rows, cols), PAIR, 0, 0, tiled=True)
    got = vmem_call(sum_body, struct((zh * own_rows, cols), BF16))(got)
    got = lax.all_to_all(got.reshape(zh, own_rows, cols), "zh", 0, 0, tiled=True)
    got = vmem_call(sum_body, struct((own_rows, cols), F32))(got)
    both = lax.all_gather(got, "c", axis=0, tiled=True)

    return pl.pallas_call(
        focused_body,
        out_shape=struct((steps, focal_here, cols), BF16),
        in_specs=[pl.BlockSpec(memory_space=pltpu.VMEM)] * 2,
        out_specs=pl.BlockSpec(memory_space=pltpu.HBM),
        scratch_shapes=[pltpu.VMEM(f_time.shape, BF16), pltpu.SemaphoreType.DMA((2,))],
        compiler_params=pltpu.CompilerParams(vmem_limit_bytes=12 << 20),
    )(table, both)


def solution(mesh):
    src, rcv, frq = (mesh.shape[a] for a in ("src", "rcv", "frq"))
    devices = mesh.devices.reshape(src // 4, 2, 2, rcv // 2, 2, frq)
    return jax.shard_map(
        shards,
        mesh=Mesh(devices, SRC + RCV + ("c",)),
        in_specs=(P("c", SRC, RCV), P(None, "c", SRC, RCV), P(SRC, RCV), P()),
        out_specs=P("c", SRC, RCV),
        check_vma=False,
    )
```

```python
import math

import jax
import jax.numpy as jnp
from jax import lax
from jax.experimental import pallas as pl
from jax.experimental.pallas import tpu as pltpu
from jax.sharding import Mesh, PartitionSpec as P

NT = 512
FREQ = 8
HALF = FREQ // 2
LANES = 128
HIGHEST = lax.Precision.HIGHEST
BF16 = jnp.bfloat16
F32 = jnp.float32
SRC = ("zh", "zl", "xl")
RCV = ("y", "xh")
PAIR = ("zl", "xl")
ROWS = 2 * HALF


def iota(shape, axis):
    return lax.broadcasted_iota(jnp.int32, shape, axis)


def wave(freq_ids, parts, sample_ids):
    phase = ((1 + freq_ids * NT // (2 * FREQ)) * sample_ids + parts * (NT // 4)) % NT
    return jnp.cos(phase.astype(F32) * (2.0 * math.pi / NT))


def thirds(x):
    high = x.astype(BF16)
    rest = x - high.astype(F32)
    middle = rest.astype(BF16)
    return high, middle, (rest - middle.astype(F32)).astype(BF16)


def vmem_call(body, out_shape, scratch=(), cost=None):
    return pl.pallas_call(
        body,
        out_shape=out_shape,
        scratch_shapes=list(scratch),
        cost_estimate=cost,
        compiler_params=pltpu.CompilerParams(vmem_limit_bytes=12 << 20),
    )


def far_order(count):
    step = 1 if count % 3 == 0 else 3
    return [step * j % count for j in range(count)]


def far_all_to_all(x):
    axes = SRC + RCV + ("c",)
    zh, *rest = (lax.axis_size(a) for a in axes)
    apart = math.prod(rest)
    groups = [[j * apart + i for j in far_order(zh)] for i in range(apart)]
    return lax.all_to_all(x, axes, 0, 0, tiled=True, axis_index_groups=groups)


def spectra_body(f_ref, own_ref, other_ref, last_ref, held_ref, sem_ref):
    steps, focal, cols = f_ref.shape
    pieces = sem_ref.shape[0]
    block = steps // pieces
    copies = []
    for i in range(pieces):
        at = pl.ds(i * block, block)
        copies.append(pltpu.make_async_copy(f_ref.at[at], held_ref.at[at], sem_ref.at[i]))
        copies[-1].start()
    core = lax.axis_index("c")
    table = focal_table((core, 1 - core), core, steps, focal, 1.0 / math.sqrt(NT))
    rows = table.shape[0]
    table = jnp.concatenate(thirds(table), 0)
    high, middle, low = thirds(focal_table((0, 1), core, steps, focal, 1.0 / math.sqrt(FREQ)))
    last_ref[...] = jnp.concatenate([high, high, middle, high, low, middle], 0)
    sums = 0.0
    for i, copy in enumerate(copies):
        copy.wait()
        merged = held_ref[i * block : (i + 1) * block].reshape(block * focal, cols)
        left = table[:, i * block * focal : (i + 1) * block * focal]
        sums += jnp.dot(left, merged, preferred_element_type=F32)
    sums = sums[:rows] + sums[rows : 2 * rows] + sums[2 * rows :]
    own_ref[...] = sums[: rows // 2]
    other_ref[...] = sums[rows // 2 :]


def masked_body(band_ref, resp_ref, out_ref):
    band = band_ref[...].astype(F32).astype(BF16)
    down, across = band.shape
    parts, _, sources, cols = resp_ref.shape
    shape = (across, cols)
    picks = (iota(shape, 0) == iota(shape, 1) // (cols // across)).astype(F32).astype(BF16)
    wide = jnp.dot(band, picks, preferred_element_type=F32).astype(BF16)
    shape = (sources, down)
    picks = (iota(shape, 0) // (sources // down) == iota(shape, 1)).astype(F32).astype(BF16)
    mask = jnp.dot(picks, wide, preferred_element_type=F32).astype(BF16)
    for c in range(parts):
        for k in range(HALF):
            out_ref[c, k] = resp_ref[c, k] * mask


def forward_body(spec_ref, resp_ref, out_ref, wide_ref, sums_ref):
    blocks = wide_ref.shape[0]
    points = spec_ref.shape[0] // ROWS
    chunks, _, lanes = out_ref.shape
    for j in range(blocks):
        wide_ref[j] = spec_ref[:, j * lanes : (j + 1) * lanes].astype(F32)

    def pick(row):
        pieces = [wide_ref[j, pl.ds(row, points, stride=ROWS), :] for j in range(blocks)]
        return jnp.concatenate(pieces, 1)

    for k in range(HALF):
        real, imag = pick(k), pick(HALF + k)
        first = jnp.concatenate([real, imag], 0).astype(BF16)
        second = jnp.concatenate([-imag, real], 0).astype(BF16)
        dims = (((1,), (1,)), ((), ()))
        sums = lax.dot_general(first, resp_ref[0, k], dims, preferred_element_type=F32)
        sums += lax.dot_general(second, resp_ref[1, k], dims, preferred_element_type=F32)
        head = sums[:, :lanes]
        rest = sums[:, lanes:]
        tail = jnp.concatenate(
            [rest, jnp.zeros((rest.shape[0], lanes - rest.shape[1]), F32)], 1
        )
        for part in range(2):
            at = pl.ds(part * HALF + k, points, stride=ROWS)
            sums_ref[0, at, :] = head[part * points : (part + 1) * points]
            sums_ref[1, at, :] = tail[part * points : (part + 1) * points]
    rows = points * ROWS // chunks
    for d in range(chunks):
        out_ref[d, :rows] = sums_ref[0, d * rows : (d + 1) * rows]
        tail = sums_ref[1, d * rows : (d + 1) * rows]
        out_ref[d, rows:] = tail[: rows // 2] + pltpu.roll(tail[rows // 2 :], lanes // 2, 1)


def gate_body(matrix_ref, parts_ref, out_ref):
    chunks, packed, lanes = parts_ref.shape
    rows = packed * 2 // 3
    cores = []
    for f in range(2):
        total = parts_ref[f]
        for d in range(f + 2, chunks, 2):
            total += parts_ref[d]
        tail = total[rows:]
        tail = jnp.concatenate([tail[:, : lanes // 2], tail[:, lanes // 2 :]], 0)
        cores.append(jnp.concatenate([total[:rows], tail], 1))
    gated = jnp.dot(
        matrix_ref[...], jnp.concatenate(cores, 0), precision=HIGHEST, preferred_element_type=F32
    ).astype(BF16)
    for f in range(2):
        mine = gated[f * rows : (f + 1) * rows]
        tail = mine[:, lanes:]
        tail = jnp.concatenate([tail[: rows // 2], tail[rows // 2 :]], 1)
        mine = jnp.concatenate([mine[:, :lanes], tail], 0)
        for d in range(f, chunks, 2):
            out_ref[d] = mine


def adjoint_body(win_ref, resp_ref, out_ref, wide_ref, sums_ref):
    chunks, packed, lanes = win_ref.shape
    rows = packed * 2 // 3
    points = chunks * rows // ROWS
    sources = resp_ref.shape[2]
    blocks = sums_ref.shape[0]
    for d in range(chunks):
        wide_ref[0, d * rows : (d + 1) * rows] = win_ref[d, :rows].astype(F32)
        tail = win_ref[d, rows:].astype(F32)
        half = d * rows + rows // 2
        wide_ref[1, d * rows : half] = tail
        wide_ref[1, half : (d + 1) * rows] = pltpu.roll(tail, lanes // 2, 1)

    def pick(row):
        pieces = [wide_ref[j, pl.ds(row, points, stride=ROWS), :] for j in range(2)]
        return jnp.concatenate(pieces, 1)[:, :sources]

    for k in range(HALF):
        real, imag = pick(k), pick(HALF + k)
        first = jnp.concatenate([real, imag], 0).astype(BF16)
        second = jnp.concatenate([imag, -real], 0).astype(BF16)
        sums = jnp.dot(first, resp_ref[0, k], preferred_element_type=F32)
        sums += jnp.dot(second, resp_ref[1, k], preferred_element_type=F32)
        for part in range(2):
            at = pl.ds(part * HALF + k, points, stride=ROWS)
            for j in range(blocks):
                sums_ref[j, at, :] = sums[
                    part * points : (part + 1) * points, j * lanes : (j + 1) * lanes
                ]
    for j in range(blocks):
        out_ref[:, j * lanes : (j + 1) * lanes] = sums_ref[j].astype(BF16)


def sum_body(got_ref, out_ref):
    total = got_ref[0].astype(F32)
    for d in range(1, got_ref.shape[0]):
        total += got_ref[d].astype(F32)
    out_ref[...] = total.astype(out_ref.dtype)


def focused_body(table_ref, sums_ref, out_ref, held_ref, sem_ref):
    steps, focal, cols = out_ref.shape
    high, middle, low = thirds(sums_ref[...])
    right = jnp.concatenate([high, middle, high, low, high, middle], 0)
    dims = (((0,), (0,)), ((), ()))
    pieces = sem_ref.shape[0]
    block = steps // pieces
    copies = []
    for i in range(pieces):
        left = table_ref[:, i * block * focal : (i + 1) * block * focal]
        values = lax.dot_general(left, right, dims, preferred_element_type=F32)
        at = pl.ds(i * block, block)
        held_ref[at] = values.astype(BF16).reshape(block, focal, cols)
        copies.append(pltpu.make_async_copy(held_ref.at[at], out_ref.at[at], sem_ref.at[i]))
        copies[-1].start()
    for copy in copies:
        copy.wait()


def focal_table(core_ids, core, steps, focal, scale):
    shape = (2 * focal * ROWS, steps * focal)
    row, col = iota(shape, 0), iota(shape, 1)
    held = jnp.where(row < focal * ROWS, core_ids[0], core_ids[1])
    table = wave(held * HALF + row % HALF, row // HALF % 2, core * steps + col // focal)
    return jnp.where(row // ROWS % focal == col % focal, table * scale, 0.0)


def shards(f_time, reflect, band_map, gates):
    steps, focal_here, cols = f_time.shape
    sources = reflect.shape[2]
    zh, zl, xl = (lax.axis_size(a) for a in SRC)
    pairs = zl * xl
    n_rcv = lax.axis_size(RCV)
    chunks = 2 * n_rcv
    focal = zh * pairs * focal_here
    core = lax.axis_index("c")
    own_rows = focal_here * ROWS
    struct = jax.ShapeDtypeStruct

    own, other, table = pl.pallas_call(
        spectra_body,
        out_shape=[struct((own_rows, cols), F32)] * 2
        + [struct((6 * 2 * own_rows, steps * focal_here), BF16)],
        in_specs=[pl.BlockSpec(memory_space=pltpu.HBM)],
        scratch_shapes=[pltpu.VMEM(f_time.shape, BF16), pltpu.SemaphoreType.DMA((4,))],
        compiler_params=pltpu.CompilerParams(vmem_limit_bytes=54784 << 10),
    )(f_time)
    others = lax.all_gather(other, "c", axis=0)
    others, core, gates, band_map = lax.optimization_barrier((others, core, gates, band_map))
    other = jnp.where(core == 0, others[1], others[0])
    spectra = (own + other).astype(BF16)
    near = jnp.broadcast_to(spectra[None], (zh, own_rows, cols))
    near = far_all_to_all(near).reshape(zh * own_rows, cols)

    masked = vmem_call(
        masked_body,
        struct(reflect.shape, BF16),
        cost=pl.CostEstimate(flops=reflect.size, transcendentals=0, bytes_accessed=4 * reflect.size),
    )(band_map, reflect)

    part_rows = focal * ROWS // chunks
    part_focal = part_rows // ROWS
    shape = (2 * part_rows, NT)
    row, col = iota(shape, 0), iota(shape, 1)
    waves = wave(row // part_rows * HALF + row % HALF, row // HALF % 2, col)
    point = (lax.axis_index(RCV) * 2 + core) * part_focal + iota((2 * part_rows, focal), 0) // ROWS % part_focal
    block = point // focal_here
    far = block % zh * far_order(zh)[1] % zh
    point = (far * pairs + block // zh) * focal_here + point % focal_here
    window = jnp.where(point == iota((2 * part_rows, focal), 1), gates[None, :], 0).sum(1)
    inner = jnp.where(col < window[:, None], waves / math.sqrt(NT), 0.0)
    matrix = lax.dot_general(
        inner, waves * (2.0 / math.sqrt(NT)), (((1,), (1,)), ((), ())), precision=HIGHEST
    )
    shape = matrix.shape
    same = iota(shape, 0) // ROWS % part_focal == iota(shape, 1) // ROWS % part_focal
    matrix = jnp.where(same, matrix, 0.0)
    near, masked, matrix = lax.optimization_barrier((near, masked, matrix))
    every = jnp.broadcast_to(near[None], (pairs, zh * own_rows, cols))
    every = lax.all_to_all(every, PAIR, 0, 0, tiled=True).reshape(focal * ROWS, cols)

    packed = part_rows * 3 // 2
    parts = vmem_call(
        forward_body,
        struct((chunks, packed, LANES), F32),
        [
            pltpu.VMEM((cols // LANES, focal * ROWS, LANES), F32),
            pltpu.VMEM((2, focal * ROWS, LANES), F32),
        ],
    )(every, masked)
    parts = lax.all_to_all(parts, RCV + ("c",), 0, 0, tiled=True)

    gated = vmem_call(gate_body, struct((chunks, packed, LANES), BF16))(matrix, parts)
    windowed = lax.all_to_all(gated, RCV + ("c",), 0, 0, tiled=True)

    sends = vmem_call(
        adjoint_body,
        struct((focal * ROWS, cols), BF16),
        [
            pltpu.VMEM((2, focal * ROWS, LANES), F32),
            pltpu.VMEM((cols // LANES, focal * ROWS, LANES), F32),
        ],
    )(windowed, masked)
    got = lax.all_to_all(sends.reshape(pairs, zh * own_rows, cols), PAIR, 0, 0, tiled=True)
    got = vmem_call(sum_body, struct((zh * own_rows, cols), BF16))(got)
    got = far_all_to_all(got.reshape(zh, own_rows, cols))
    got = vmem_call(sum_body, struct((own_rows, cols), F32))(got)
    both = lax.all_gather(got, "c", axis=0, tiled=True)

    return pl.pallas_call(
        focused_body,
        out_shape=struct((steps, focal_here, cols), BF16),
        in_specs=[pl.BlockSpec(memory_space=pltpu.VMEM)] * 2,
        out_specs=pl.BlockSpec(memory_space=pltpu.HBM),
        scratch_shapes=[pltpu.VMEM(f_time.shape, BF16), pltpu.SemaphoreType.DMA((4,))],
        compiler_params=pltpu.CompilerParams(vmem_limit_bytes=12 << 20),
    )(table, both)


def solution(mesh):
    src, rcv, frq = (mesh.shape[a] for a in ("src", "rcv", "frq"))
    devices = mesh.devices.reshape(src // 4, 2, 2, rcv // 2, 2, frq)
    return jax.shard_map(
        shards,
        mesh=Mesh(devices, SRC + RCV + ("c",)),
        in_specs=(P("c", SRC, RCV), P(None, "c", SRC, RCV), P(SRC, RCV), P()),
        out_specs=P("c", SRC, RCV),
        check_vma=False,
    )
```

```python
import math

import jax
import jax.numpy as jnp
from jax import lax
from jax.experimental import pallas as pl
from jax.experimental.pallas import tpu as pltpu
from jax.sharding import Mesh, PartitionSpec as P

NT = 512
FREQ = 8
HALF = FREQ // 2
LANES = 128
HIGHEST = lax.Precision.HIGHEST
BF16 = jnp.bfloat16
F32 = jnp.float32
SRC = ("zh", "zl", "xl")
RCV = ("y", "xh")
PAIR = ("zl", "xl")
ROWS = 2 * HALF


def iota(shape, axis):
    return lax.broadcasted_iota(jnp.int32, shape, axis)


def wave(freq_ids, parts, sample_ids):
    phase = ((1 + freq_ids * NT // (2 * FREQ)) * sample_ids + parts * (NT // 4)) % NT
    return jnp.cos(phase.astype(F32) * (2.0 * math.pi / NT))


def thirds(x):
    high = x.astype(BF16)
    rest = x - high.astype(F32)
    middle = rest.astype(BF16)
    return high, middle, (rest - middle.astype(F32)).astype(BF16)


def vmem_call(body, out_shape, scratch=(), cost=None):
    return pl.pallas_call(
        body,
        out_shape=out_shape,
        scratch_shapes=list(scratch),
        cost_estimate=cost,
        compiler_params=pltpu.CompilerParams(vmem_limit_bytes=12 << 20),
    )


def far_order(count):
    step = 1 if count % 5 == 0 else 5
    return [step * j % count for j in range(count)]


def far_all_to_all(x):
    axes = SRC + RCV + ("c",)
    zh, *rest = (lax.axis_size(a) for a in axes)
    apart = math.prod(rest)
    groups = [[j * apart + i for j in far_order(zh)] for i in range(apart)]
    return lax.all_to_all(x, axes, 0, 0, tiled=True, axis_index_groups=groups)


def spectra_body(f_ref, own_ref, other_ref, last_ref, held_ref, sem_ref):
    steps, focal, cols = f_ref.shape
    pieces = sem_ref.shape[0]
    block = steps // pieces
    copies = []
    for i in range(pieces):
        at = pl.ds(i * block, block)
        copies.append(pltpu.make_async_copy(f_ref.at[at], held_ref.at[at], sem_ref.at[i]))
        copies[-1].start()
    core = lax.axis_index("c")
    table = focal_table((core, 1 - core), core, steps, focal, 1.0 / math.sqrt(NT))
    rows = table.shape[0]
    table = jnp.concatenate(thirds(table), 0)
    high, middle, low = thirds(focal_table((0, 1), core, steps, focal, 1.0 / math.sqrt(FREQ)))
    last_ref[...] = jnp.concatenate([high, high, middle, high, low, middle], 0)
    sums = 0.0
    for i, copy in enumerate(copies):
        copy.wait()
        merged = held_ref[i * block : (i + 1) * block].reshape(block * focal, cols)
        left = table[:, i * block * focal : (i + 1) * block * focal]
        sums += jnp.dot(left, merged, preferred_element_type=F32)
    sums = sums[:rows] + sums[rows : 2 * rows] + sums[2 * rows :]
    own_ref[...] = sums[: rows // 2]
    other_ref[...] = sums[rows // 2 :]


def local_body(band_ref, gates_ref, resp_ref, masked_ref, matrix_ref):
    across, down = band_ref.shape
    parts, _, sources, cols = resp_ref.shape
    shape = (across, cols)
    picks = (iota(shape, 0) == iota(shape, 1) // (cols // across)).astype(F32).astype(BF16)
    band = band_ref[...].astype(F32).astype(BF16)
    dims = (((0,), (0,)), ((), ()))
    wide = lax.dot_general(band, picks, dims, preferred_element_type=F32).astype(BF16)
    shape = (sources, down)
    picks = (iota(shape, 0) // (sources // down) == iota(shape, 1)).astype(F32).astype(BF16)
    mask = jnp.dot(picks, wide, preferred_element_type=F32).astype(BF16)
    for c in range(parts):
        for k in range(HALF):
            masked_ref[c, k] = resp_ref[c, k] * mask

    zh, zl, xl = (lax.axis_size(a) for a in SRC)
    focal = gates_ref.shape[1]
    pairs, focal_here = zl * xl, focal // (zh * zl * xl)
    rows = matrix_ref.shape[0]
    part_focal = rows // (2 * ROWS)
    shape = (rows, NT)
    row, col = iota(shape, 0), iota(shape, 1)
    waves = wave(row // (rows // 2) * HALF + row % HALF, row // HALF % 2, col)
    chunk = lax.axis_index("y") * lax.axis_size("xh") + lax.axis_index("xh")
    chunk = chunk * 2 + lax.axis_index("c")
    shape = (rows, focal)
    point = chunk * part_focal + iota(shape, 0) // ROWS % part_focal
    block = point // focal_here
    far = block % zh * far_order(zh)[1] % zh
    point = (far * pairs + block // zh) * focal_here + point % focal_here
    own = jnp.where(point == iota(shape, 1), gates_ref[...].astype(F32), 0.0)
    window = jnp.sum(own, 1, keepdims=True)
    inner = jnp.where(col.astype(F32) < window, waves / math.sqrt(NT), 0.0)
    matrix = lax.dot_general(
        inner,
        waves * (2.0 / math.sqrt(NT)),
        (((1,), (1,)), ((), ())),
        precision=HIGHEST,
        preferred_element_type=F32,
    )
    shape = matrix.shape
    same = iota(shape, 0) // ROWS % part_focal == iota(shape, 1) // ROWS % part_focal
    matrix_ref[...] = jnp.where(same, matrix, 0.0)


def forward_body(spec_ref, resp_ref, out_ref, wide_ref, sums_ref):
    blocks = wide_ref.shape[0]
    points = spec_ref.shape[0] // ROWS
    chunks, _, lanes = out_ref.shape
    for j in range(blocks):
        wide_ref[j] = spec_ref[:, j * lanes : (j + 1) * lanes].astype(F32)

    def pick(row):
        pieces = [wide_ref[j, pl.ds(row, points, stride=ROWS), :] for j in range(blocks)]
        return jnp.concatenate(pieces, 1)

    for k in range(HALF):
        real, imag = pick(k), pick(HALF + k)
        first = jnp.concatenate([real, imag], 0).astype(BF16)
        second = jnp.concatenate([-imag, real], 0).astype(BF16)
        dims = (((1,), (1,)), ((), ()))
        sums = lax.dot_general(first, resp_ref[0, k], dims, preferred_element_type=F32)
        sums += lax.dot_general(second, resp_ref[1, k], dims, preferred_element_type=F32)
        head = sums[:, :lanes]
        rest = sums[:, lanes:]
        tail = jnp.concatenate(
            [rest, jnp.zeros((rest.shape[0], lanes - rest.shape[1]), F32)], 1
        )
        for part in range(2):
            at = pl.ds(part * HALF + k, points, stride=ROWS)
            sums_ref[0, at, :] = head[part * points : (part + 1) * points]
            sums_ref[1, at, :] = tail[part * points : (part + 1) * points]
    rows = points * ROWS // chunks
    for d in range(chunks):
        out_ref[d, :rows] = sums_ref[0, d * rows : (d + 1) * rows]
        tail = sums_ref[1, d * rows : (d + 1) * rows]
        out_ref[d, rows:] = tail[: rows // 2] + pltpu.roll(tail[rows // 2 :], lanes // 2, 1)


def gate_body(matrix_ref, parts_ref, out_ref):
    chunks, packed, lanes = parts_ref.shape
    rows = packed * 2 // 3
    cores = []
    for f in range(2):
        total = parts_ref[f]
        for d in range(f + 2, chunks, 2):
            total += parts_ref[d]
        tail = total[rows:]
        tail = jnp.concatenate([tail[:, : lanes // 2], tail[:, lanes // 2 :]], 0)
        cores.append(jnp.concatenate([total[:rows], tail], 1))
    gated = jnp.dot(
        matrix_ref[...], jnp.concatenate(cores, 0), precision=HIGHEST, preferred_element_type=F32
    ).astype(BF16)
    for f in range(2):
        mine = gated[f * rows : (f + 1) * rows]
        tail = mine[:, lanes:]
        tail = jnp.concatenate([tail[: rows // 2], tail[rows // 2 :]], 1)
        mine = jnp.concatenate([mine[:, :lanes], tail], 0)
        for d in range(f, chunks, 2):
            out_ref[d] = mine


def adjoint_body(win_ref, resp_ref, out_ref, wide_ref, sums_ref):
    chunks, packed, lanes = win_ref.shape
    rows = packed * 2 // 3
    points = chunks * rows // ROWS
    sources = resp_ref.shape[2]
    blocks = sums_ref.shape[0]
    for d in range(chunks):
        wide_ref[0, d * rows : (d + 1) * rows] = win_ref[d, :rows].astype(F32)
        tail = win_ref[d, rows:].astype(F32)
        half = d * rows + rows // 2
        wide_ref[1, d * rows : half] = tail
        wide_ref[1, half : (d + 1) * rows] = pltpu.roll(tail, lanes // 2, 1)

    def pick(row):
        pieces = [wide_ref[j, pl.ds(row, points, stride=ROWS), :] for j in range(2)]
        return jnp.concatenate(pieces, 1)[:, :sources]

    for k in range(HALF):
        real, imag = pick(k), pick(HALF + k)
        first = jnp.concatenate([real, imag], 0).astype(BF16)
        second = jnp.concatenate([imag, -real], 0).astype(BF16)
        sums = jnp.dot(first, resp_ref[0, k], preferred_element_type=F32)
        sums += jnp.dot(second, resp_ref[1, k], preferred_element_type=F32)
        for part in range(2):
            at = pl.ds(part * HALF + k, points, stride=ROWS)
            for j in range(blocks):
                sums_ref[j, at, :] = sums[
                    part * points : (part + 1) * points, j * lanes : (j + 1) * lanes
                ]
    for j in range(blocks):
        out_ref[:, j * lanes : (j + 1) * lanes] = sums_ref[j].astype(BF16)


def sum_body(got_ref, out_ref):
    total = got_ref[0].astype(F32)
    for d in range(1, got_ref.shape[0]):
        total += got_ref[d].astype(F32)
    out_ref[...] = total.astype(out_ref.dtype)


def focused_body(table_ref, sums_ref, out_ref, held_ref, sem_ref):
    steps, focal, cols = out_ref.shape
    high, middle, low = thirds(sums_ref[...])
    right = jnp.concatenate([high, middle, high, low, high, middle], 0)
    dims = (((0,), (0,)), ((), ()))
    pieces = sem_ref.shape[0]
    block = steps // pieces
    copies = []
    for i in range(pieces):
        left = table_ref[:, i * block * focal : (i + 1) * block * focal]
        values = lax.dot_general(left, right, dims, preferred_element_type=F32)
        at = pl.ds(i * block, block)
        held_ref[at] = values.astype(BF16).reshape(block, focal, cols)
        copies.append(pltpu.make_async_copy(held_ref.at[at], out_ref.at[at], sem_ref.at[i]))
        copies[-1].start()
    for copy in copies:
        copy.wait()


def focal_table(core_ids, core, steps, focal, scale):
    shape = (2 * focal * ROWS, steps * focal)
    row, col = iota(shape, 0), iota(shape, 1)
    held = jnp.where(row < focal * ROWS, core_ids[0], core_ids[1])
    table = wave(held * HALF + row % HALF, row // HALF % 2, core * steps + col // focal)
    return jnp.where(row // ROWS % focal == col % focal, table * scale, 0.0)


def shards(f_time, reflect, band_map, gates):
    steps, focal_here, cols = f_time.shape
    sources = reflect.shape[2]
    zh, zl, xl = (lax.axis_size(a) for a in SRC)
    pairs = zl * xl
    n_rcv = lax.axis_size(RCV)
    chunks = 2 * n_rcv
    focal = zh * pairs * focal_here
    core = lax.axis_index("c")
    own_rows = focal_here * ROWS
    struct = jax.ShapeDtypeStruct

    own, other, table = pl.pallas_call(
        spectra_body,
        out_shape=[struct((own_rows, cols), F32)] * 2
        + [struct((6 * 2 * own_rows, steps * focal_here), BF16)],
        in_specs=[pl.BlockSpec(memory_space=pltpu.HBM)],
        scratch_shapes=[pltpu.VMEM(f_time.shape, BF16), pltpu.SemaphoreType.DMA((4,))],
        compiler_params=pltpu.CompilerParams(vmem_limit_bytes=54784 << 10),
    )(f_time)
    others = lax.all_gather(other, "c", axis=0)
    other = jnp.where(core == 0, others[1], others[0])
    spectra = (own + other).astype(BF16)
    near = jnp.broadcast_to(spectra[None], (zh, own_rows, cols))
    near = far_all_to_all(near).reshape(zh * own_rows, cols)
    every = jnp.broadcast_to(near[None], (pairs, zh * own_rows, cols))
    every = lax.all_to_all(every, PAIR, 0, 0, tiled=True).reshape(focal * ROWS, cols)
    every, gates, band_map = lax.optimization_barrier((every, gates, band_map))
    part_rows = focal * ROWS // chunks
    masked, matrix = vmem_call(
        local_body, [struct(reflect.shape, BF16), struct((2 * part_rows, 2 * part_rows), F32)]
    )(band_map.T, gates.reshape(1, focal), reflect)

    packed = part_rows * 3 // 2
    parts = vmem_call(
        forward_body,
        struct((chunks, packed, LANES), F32),
        [
            pltpu.VMEM((cols // LANES, focal * ROWS, LANES), F32),
            pltpu.VMEM((2, focal * ROWS, LANES), F32),
        ],
    )(every, masked)
    parts = lax.all_to_all(parts, RCV + ("c",), 0, 0, tiled=True)

    gated = vmem_call(gate_body, struct((chunks, packed, LANES), BF16))(matrix, parts)
    windowed = lax.all_to_all(gated, RCV + ("c",), 0, 0, tiled=True)

    sends = vmem_call(
        adjoint_body,
        struct((focal * ROWS, cols), BF16),
        [
            pltpu.VMEM((2, focal * ROWS, LANES), F32),
            pltpu.VMEM((cols // LANES, focal * ROWS, LANES), F32),
        ],
    )(windowed, masked)
    got = lax.all_to_all(sends.reshape(pairs, zh * own_rows, cols), PAIR, 0, 0, tiled=True)
    got = vmem_call(sum_body, struct((zh * own_rows, cols), BF16))(got)
    got = far_all_to_all(got.reshape(zh, own_rows, cols))
    got = vmem_call(sum_body, struct((own_rows, cols), F32))(got)
    both = lax.all_gather(got, "c", axis=0, tiled=True)

    return pl.pallas_call(
        focused_body,
        out_shape=struct((steps, focal_here, cols), BF16),
        in_specs=[pl.BlockSpec(memory_space=pltpu.VMEM)] * 2,
        out_specs=pl.BlockSpec(memory_space=pltpu.HBM),
        scratch_shapes=[pltpu.VMEM(f_time.shape, BF16), pltpu.SemaphoreType.DMA((4,))],
        compiler_params=pltpu.CompilerParams(vmem_limit_bytes=12 << 20),
    )(table, both)


def solution(mesh):
    src, rcv, frq = (mesh.shape[a] for a in ("src", "rcv", "frq"))
    devices = mesh.devices.reshape(src // 4, 2, 2, rcv // 2, 2, frq)
    return jax.shard_map(
        shards,
        mesh=Mesh(devices, SRC + RCV + ("c",)),
        in_specs=(P("c", SRC, RCV), P(None, "c", SRC, RCV), P(SRC, RCV), P()),
        out_specs=P("c", SRC, RCV),
        check_vma=False,
    )
```

```python
import math

import jax
import jax.numpy as jnp
from jax import lax
from jax.experimental import pallas as pl
from jax.experimental.pallas import tpu as pltpu
from jax.sharding import Mesh, PartitionSpec as P

NT = 512
FREQ = 8
HALF = FREQ // 2
LANES = 128
HIGHEST = lax.Precision.HIGHEST
BF16 = jnp.bfloat16
F32 = jnp.float32
SRC = ("zh", "zl", "xl")
RCV = ("y", "xh")
PAIR = ("zl", "xl")
ROWS = 2 * HALF


def iota(shape, axis):
    return lax.broadcasted_iota(jnp.int32, shape, axis)


def wave(freq_ids, parts, sample_ids):
    phase = ((1 + freq_ids * NT // (2 * FREQ)) * sample_ids + parts * (NT // 4)) % NT
    return jnp.cos(phase.astype(F32) * (2.0 * math.pi / NT))


def thirds(x):
    high = x.astype(BF16)
    rest = x - high.astype(F32)
    middle = rest.astype(BF16)
    return high, middle, (rest - middle.astype(F32)).astype(BF16)


def vmem_call(body, out_shape, scratch=(), cost=None):
    return pl.pallas_call(
        body,
        out_shape=out_shape,
        scratch_shapes=list(scratch),
        cost_estimate=cost,
        compiler_params=pltpu.CompilerParams(vmem_limit_bytes=12 << 20),
    )


def far_order(count):
    return sorted(range(count), key=lambda j: (min(j, count - j), j))


def far_all_to_all(x):
    axes = SRC + RCV + ("c",)
    zh, *rest = (lax.axis_size(a) for a in axes)
    apart = math.prod(rest)
    groups = [[j * apart + i for j in far_order(zh)] for i in range(apart)]
    return lax.all_to_all(x, axes, 0, 0, tiled=True, axis_index_groups=groups)


def spectra_body(f_ref, own_ref, other_ref, last_ref, held_ref, sem_ref):
    steps, focal, cols = f_ref.shape
    pieces = sem_ref.shape[0]
    block = steps // pieces
    copies = []
    for i in range(pieces):
        at = pl.ds(i * block, block)
        copies.append(pltpu.make_async_copy(f_ref.at[at], held_ref.at[at], sem_ref.at[i]))
        copies[-1].start()
    core = lax.axis_index("c")
    table = focal_table((core, 1 - core), core, steps, focal, 1.0 / math.sqrt(NT))
    rows = table.shape[0]
    table = jnp.concatenate(thirds(table), 0)
    high, middle, low = thirds(focal_table((0, 1), core, steps, focal, 1.0 / math.sqrt(FREQ)))
    last_ref[...] = jnp.concatenate([high, high, middle, high, low, middle], 0)
    sums = 0.0
    for i, copy in enumerate(copies):
        copy.wait()
        merged = held_ref[i * block : (i + 1) * block].reshape(block * focal, cols)
        left = table[:, i * block * focal : (i + 1) * block * focal]
        sums += jnp.dot(left, merged, preferred_element_type=F32)
    sums = sums[:rows] + sums[rows : 2 * rows] + sums[2 * rows :]
    own_ref[...] = sums[: rows // 2]
    other_ref[...] = sums[rows // 2 :]


def masked_body(band_ref, resp_ref, out_ref):
    band = band_ref[...].astype(F32).astype(BF16)
    down, across = band.shape
    parts, _, sources, cols = resp_ref.shape
    shape = (across, cols)
    picks = (iota(shape, 0) == iota(shape, 1) // (cols // across)).astype(F32).astype(BF16)
    wide = jnp.dot(band, picks, preferred_element_type=F32).astype(BF16)
    shape = (sources, down)
    picks = (iota(shape, 0) // (sources // down) == iota(shape, 1)).astype(F32).astype(BF16)
    mask = jnp.dot(picks, wide, preferred_element_type=F32).astype(BF16)
    for c in range(parts):
        for k in range(HALF):
            out_ref[c, k] = resp_ref[c, k] * mask


def forward_body(spec_ref, resp_ref, out_ref, wide_ref, sums_ref):
    blocks = wide_ref.shape[0]
    points = spec_ref.shape[0] // ROWS
    chunks, _, lanes = out_ref.shape
    for j in range(blocks):
        wide_ref[j] = spec_ref[:, j * lanes : (j + 1) * lanes].astype(F32)

    def pick(row):
        pieces = [wide_ref[j, pl.ds(row, points, stride=ROWS), :] for j in range(blocks)]
        return jnp.concatenate(pieces, 1)

    for k in range(HALF):
        real, imag = pick(k), pick(HALF + k)
        first = jnp.concatenate([real, imag], 0).astype(BF16)
        second = jnp.concatenate([-imag, real], 0).astype(BF16)
        dims = (((1,), (1,)), ((), ()))
        sums = lax.dot_general(first, resp_ref[0, k], dims, preferred_element_type=F32)
        sums += lax.dot_general(second, resp_ref[1, k], dims, preferred_element_type=F32)
        head = sums[:, :lanes]
        rest = sums[:, lanes:]
        tail = jnp.concatenate(
            [rest, jnp.zeros((rest.shape[0], lanes - rest.shape[1]), F32)], 1
        )
        for part in range(2):
            at = pl.ds(part * HALF + k, points, stride=ROWS)
            sums_ref[0, at, :] = head[part * points : (part + 1) * points]
            sums_ref[1, at, :] = tail[part * points : (part + 1) * points]
    rows = points * ROWS // chunks
    for d in range(chunks):
        out_ref[d, :rows] = sums_ref[0, d * rows : (d + 1) * rows]
        tail = sums_ref[1, d * rows : (d + 1) * rows]
        out_ref[d, rows:] = tail[: rows // 2] + pltpu.roll(tail[rows // 2 :], lanes // 2, 1)


def gate_body(matrix_ref, parts_ref, out_ref):
    chunks, packed, lanes = parts_ref.shape
    rows = packed * 2 // 3
    cores = []
    for f in range(2):
        total = parts_ref[f]
        for d in range(f + 2, chunks, 2):
            total += parts_ref[d]
        tail = total[rows:]
        tail = jnp.concatenate([tail[:, : lanes // 2], tail[:, lanes // 2 :]], 0)
        cores.append(jnp.concatenate([total[:rows], tail], 1))
    gated = jnp.dot(
        matrix_ref[...], jnp.concatenate(cores, 0), precision=HIGHEST, preferred_element_type=F32
    ).astype(BF16)
    for f in range(2):
        mine = gated[f * rows : (f + 1) * rows]
        tail = mine[:, lanes:]
        tail = jnp.concatenate([tail[: rows // 2], tail[rows // 2 :]], 1)
        mine = jnp.concatenate([mine[:, :lanes], tail], 0)
        for d in range(f, chunks, 2):
            out_ref[d] = mine


def adjoint_body(win_ref, resp_ref, out_ref, wide_ref, sums_ref):
    chunks, packed, lanes = win_ref.shape
    rows = packed * 2 // 3
    points = chunks * rows // ROWS
    sources = resp_ref.shape[2]
    blocks = sums_ref.shape[0]
    for d in range(chunks):
        wide_ref[0, d * rows : (d + 1) * rows] = win_ref[d, :rows].astype(F32)
        tail = win_ref[d, rows:].astype(F32)
        half = d * rows + rows // 2
        wide_ref[1, d * rows : half] = tail
        wide_ref[1, half : (d + 1) * rows] = pltpu.roll(tail, lanes // 2, 1)

    def pick(row):
        pieces = [wide_ref[j, pl.ds(row, points, stride=ROWS), :] for j in range(2)]
        return jnp.concatenate(pieces, 1)[:, :sources]

    for k in range(HALF):
        real, imag = pick(k), pick(HALF + k)
        first = jnp.concatenate([real, imag], 0).astype(BF16)
        second = jnp.concatenate([imag, -real], 0).astype(BF16)
        sums = jnp.dot(first, resp_ref[0, k], preferred_element_type=F32)
        sums += jnp.dot(second, resp_ref[1, k], preferred_element_type=F32)
        for part in range(2):
            at = pl.ds(part * HALF + k, points, stride=ROWS)
            for j in range(blocks):
                sums_ref[j, at, :] = sums[
                    part * points : (part + 1) * points, j * lanes : (j + 1) * lanes
                ]
    for j in range(blocks):
        out_ref[:, j * lanes : (j + 1) * lanes] = sums_ref[j].astype(BF16)


def sum_body(got_ref, out_ref):
    total = got_ref[0].astype(F32)
    for d in range(1, got_ref.shape[0]):
        total += got_ref[d].astype(F32)
    out_ref[...] = total.astype(out_ref.dtype)


def focused_body(table_ref, sums_ref, out_ref, held_ref, sem_ref):
    steps, focal, cols = out_ref.shape
    high, middle, low = thirds(sums_ref[...])
    right = jnp.concatenate([high, middle, high, low, high, middle], 0)
    dims = (((0,), (0,)), ((), ()))
    pieces = sem_ref.shape[0]
    block = steps // pieces
    copies = []
    for i in range(pieces):
        left = table_ref[:, i * block * focal : (i + 1) * block * focal]
        values = lax.dot_general(left, right, dims, preferred_element_type=F32)
        at = pl.ds(i * block, block)
        held_ref[at] = values.astype(BF16).reshape(block, focal, cols)
        copies.append(pltpu.make_async_copy(held_ref.at[at], out_ref.at[at], sem_ref.at[i]))
        copies[-1].start()
    for copy in copies:
        copy.wait()


def focal_table(core_ids, core, steps, focal, scale):
    shape = (2 * focal * ROWS, steps * focal)
    row, col = iota(shape, 0), iota(shape, 1)
    held = jnp.where(row < focal * ROWS, core_ids[0], core_ids[1])
    table = wave(held * HALF + row % HALF, row // HALF % 2, core * steps + col // focal)
    return jnp.where(row // ROWS % focal == col % focal, table * scale, 0.0)


def shards(f_time, reflect, band_map, gates):
    steps, focal_here, cols = f_time.shape
    sources = reflect.shape[2]
    zh, zl, xl = (lax.axis_size(a) for a in SRC)
    pairs = zl * xl
    n_rcv = lax.axis_size(RCV)
    chunks = 2 * n_rcv
    focal = zh * pairs * focal_here
    core = lax.axis_index("c")
    own_rows = focal_here * ROWS
    struct = jax.ShapeDtypeStruct

    own, other, table = pl.pallas_call(
        spectra_body,
        out_shape=[struct((own_rows, cols), F32)] * 2
        + [struct((6 * 2 * own_rows, steps * focal_here), BF16)],
        in_specs=[pl.BlockSpec(memory_space=pltpu.HBM)],
        scratch_shapes=[pltpu.VMEM(f_time.shape, BF16), pltpu.SemaphoreType.DMA((4,))],
        compiler_params=pltpu.CompilerParams(vmem_limit_bytes=54784 << 10),
    )(f_time)
    others = lax.all_gather(other, "c", axis=0)
    others, core, gates, band_map = lax.optimization_barrier((others, core, gates, band_map))
    other = jnp.where(core == 0, others[1], others[0])
    spectra = (own + other).astype(BF16)
    near = jnp.broadcast_to(spectra[None], (zh, own_rows, cols))
    near = far_all_to_all(near).reshape(zh * own_rows, cols)

    masked = vmem_call(
        masked_body,
        struct(reflect.shape, BF16),
        cost=pl.CostEstimate(flops=reflect.size, transcendentals=0, bytes_accessed=4 * reflect.size),
    )(band_map, reflect)

    part_rows = focal * ROWS // chunks
    part_focal = part_rows // ROWS
    shape = (2 * part_rows, NT)
    row, col = iota(shape, 0), iota(shape, 1)
    waves = wave(row // part_rows * HALF + row % HALF, row // HALF % 2, col)
    point = (lax.axis_index(RCV) * 2 + core) * part_focal + iota((2 * part_rows, focal), 0) // ROWS % part_focal
    block = point // focal_here
    far = sum(jnp.where(block % zh == j, f, 0) for j, f in enumerate(far_order(zh)))
    point = (far * pairs + block // zh) * focal_here + point % focal_here
    window = jnp.where(point == iota((2 * part_rows, focal), 1), gates[None, :], 0).sum(1)
    inner = jnp.where(col < window[:, None], waves / math.sqrt(NT), 0.0)
    matrix = lax.dot_general(
        inner, waves * (2.0 / math.sqrt(NT)), (((1,), (1,)), ((), ())), precision=HIGHEST
    )
    shape = matrix.shape
    same = iota(shape, 0) // ROWS % part_focal == iota(shape, 1) // ROWS % part_focal
    matrix = jnp.where(same, matrix, 0.0)
    near, masked, matrix = lax.optimization_barrier((near, masked, matrix))
    every = jnp.broadcast_to(near[None], (pairs, zh * own_rows, cols))
    every = lax.all_to_all(every, PAIR, 0, 0, tiled=True).reshape(focal * ROWS, cols)

    packed = part_rows * 3 // 2
    parts = vmem_call(
        forward_body,
        struct((chunks, packed, LANES), F32),
        [
            pltpu.VMEM((cols // LANES, focal * ROWS, LANES), F32),
            pltpu.VMEM((2, focal * ROWS, LANES), F32),
        ],
    )(every, masked)
    parts = lax.all_to_all(parts, RCV + ("c",), 0, 0, tiled=True)

    gated = vmem_call(gate_body, struct((chunks, packed, LANES), BF16))(matrix, parts)
    windowed = lax.all_to_all(gated, RCV + ("c",), 0, 0, tiled=True)

    sends = vmem_call(
        adjoint_body,
        struct((focal * ROWS, cols), BF16),
        [
            pltpu.VMEM((2, focal * ROWS, LANES), F32),
            pltpu.VMEM((cols // LANES, focal * ROWS, LANES), F32),
        ],
    )(windowed, masked)
    got = lax.all_to_all(sends.reshape(pairs, zh * own_rows, cols), PAIR, 0, 0, tiled=True)
    got = vmem_call(sum_body, struct((zh * own_rows, cols), BF16))(got)
    got = far_all_to_all(got.reshape(zh, own_rows, cols))
    got = vmem_call(sum_body, struct((own_rows, cols), F32))(got)
    both = lax.all_gather(got, "c", axis=0, tiled=True)

    return pl.pallas_call(
        focused_body,
        out_shape=struct((steps, focal_here, cols), BF16),
        in_specs=[pl.BlockSpec(memory_space=pltpu.VMEM)] * 2,
        out_specs=pl.BlockSpec(memory_space=pltpu.HBM),
        scratch_shapes=[pltpu.VMEM(f_time.shape, BF16), pltpu.SemaphoreType.DMA((4,))],
        compiler_params=pltpu.CompilerParams(vmem_limit_bytes=12 << 20),
    )(table, both)


def solution(mesh):
    src, rcv, frq = (mesh.shape[a] for a in ("src", "rcv", "frq"))
    devices = mesh.devices.reshape(src // 4, 2, 2, rcv // 2, 2, frq)
    return jax.shard_map(
        shards,
        mesh=Mesh(devices, SRC + RCV + ("c",)),
        in_specs=(P("c", SRC, RCV), P(None, "c", SRC, RCV), P(SRC, RCV), P()),
        out_specs=P("c", SRC, RCV),
        check_vma=False,
    )
```

```python
import math

import jax
import jax.numpy as jnp
from jax import lax
from jax.experimental import pallas as pl
from jax.experimental.pallas import tpu as pltpu
from jax.sharding import Mesh, PartitionSpec as P

NT = 512
FREQ = 8
HALF = FREQ // 2
LANES = 128
HIGHEST = lax.Precision.HIGHEST
BF16 = jnp.bfloat16
F32 = jnp.float32
SRC = ("zh", "zl", "xl")
RCV = ("y", "xh")
PAIR = ("zl", "xl")
ROWS = 2 * HALF


def iota(shape, axis):
    return lax.broadcasted_iota(jnp.int32, shape, axis)


def wave(freq_ids, parts, sample_ids):
    phase = ((1 + freq_ids * NT // (2 * FREQ)) * sample_ids + parts * (NT // 4)) % NT
    return jnp.cos(phase.astype(F32) * (2.0 * math.pi / NT))


def thirds(x):
    high = x.astype(BF16)
    rest = x - high.astype(F32)
    middle = rest.astype(BF16)
    return high, middle, (rest - middle.astype(F32)).astype(BF16)


def vmem_call(body, out_shape, scratch=(), cost=None):
    return pl.pallas_call(
        body,
        out_shape=out_shape,
        scratch_shapes=list(scratch),
        cost_estimate=cost,
        compiler_params=pltpu.CompilerParams(vmem_limit_bytes=12 << 20),
    )


def far_order(count):
    step = 1 if count % 3 == 0 else 3
    return [step * j % count for j in range(count)]


def far_all_to_all(x):
    axes = SRC + RCV + ("c",)
    zh, *rest = (lax.axis_size(a) for a in axes)
    apart = math.prod(rest)
    groups = [[j * apart + i for j in far_order(zh)] for i in range(apart)]
    return lax.all_to_all(x, axes, 0, 0, tiled=True, axis_index_groups=groups)


def spectra_body(f_ref, own_ref, other_ref, last_ref, held_ref, sem_ref):
    steps, focal, cols = f_ref.shape
    pieces = sem_ref.shape[0]
    block = steps // pieces
    copies = []
    for i in range(pieces):
        at = pl.ds(i * block, block)
        copies.append(pltpu.make_async_copy(f_ref.at[at], held_ref.at[at], sem_ref.at[i]))
        copies[-1].start()
    core = lax.axis_index("c")
    table = focal_table((core, 1 - core), core, steps, focal, 1.0 / math.sqrt(NT))
    rows = table.shape[0]
    table = jnp.concatenate(thirds(table), 0)
    high, middle, low = thirds(focal_table((0, 1), core, steps, focal, 1.0 / math.sqrt(FREQ)))
    last_ref[...] = jnp.concatenate([high, high, middle, high, low, middle], 0)
    sums = 0.0
    for i, copy in enumerate(copies):
        copy.wait()
        merged = held_ref[i * block : (i + 1) * block].reshape(block * focal, cols)
        left = table[:, i * block * focal : (i + 1) * block * focal]
        sums += jnp.dot(left, merged, preferred_element_type=F32)
    sums = sums[:rows] + sums[rows : 2 * rows] + sums[2 * rows :]
    own_ref[...] = sums[: rows // 2]
    other_ref[...] = sums[rows // 2 :]


def near_body(own_ref, others_ref, out_ref, held_ref, sem_ref):
    core = lax.axis_index("c")
    held_ref[...] = (own_ref[...] + others_ref[1 - core]).astype(BF16)
    copies = []
    for j in range(out_ref.shape[0]):
        copies.append(pltpu.make_async_copy(held_ref, out_ref.at[j], sem_ref.at[j]))
        copies[-1].start()
    for copy in copies:
        copy.wait()


def masked_body(band_ref, resp_ref, out_ref):
    band = band_ref[...].astype(F32).astype(BF16)
    down, across = band.shape
    parts, _, sources, cols = resp_ref.shape
    shape = (across, cols)
    picks = (iota(shape, 0) == iota(shape, 1) // (cols // across)).astype(F32).astype(BF16)
    wide = jnp.dot(band, picks, preferred_element_type=F32).astype(BF16)
    shape = (sources, down)
    picks = (iota(shape, 0) // (sources // down) == iota(shape, 1)).astype(F32).astype(BF16)
    mask = jnp.dot(picks, wide, preferred_element_type=F32).astype(BF16)
    for c in range(parts):
        for k in range(HALF):
            out_ref[c, k] = resp_ref[c, k] * mask


def forward_body(spec_ref, resp_ref, out_ref, wide_ref, sums_ref):
    blocks = wide_ref.shape[0]
    points = spec_ref.shape[0] // ROWS
    chunks, _, lanes = out_ref.shape
    for j in range(blocks):
        wide_ref[j] = spec_ref[:, j * lanes : (j + 1) * lanes].astype(F32)

    def pick(row):
        pieces = [wide_ref[j, pl.ds(row, points, stride=ROWS), :] for j in range(blocks)]
        return jnp.concatenate(pieces, 1)

    for k in range(HALF):
        real, imag = pick(k), pick(HALF + k)
        first = jnp.concatenate([real, imag], 0).astype(BF16)
        second = jnp.concatenate([-imag, real], 0).astype(BF16)
        dims = (((1,), (1,)), ((), ()))
        sums = lax.dot_general(first, resp_ref[0, k], dims, preferred_element_type=F32)
        sums += lax.dot_general(second, resp_ref[1, k], dims, preferred_element_type=F32)
        head = sums[:, :lanes]
        rest = sums[:, lanes:]
        tail = jnp.concatenate(
            [rest, jnp.zeros((rest.shape[0], lanes - rest.shape[1]), F32)], 1
        )
        for part in range(2):
            at = pl.ds(part * HALF + k, points, stride=ROWS)
            sums_ref[0, at, :] = head[part * points : (part + 1) * points]
            sums_ref[1, at, :] = tail[part * points : (part + 1) * points]
    rows = points * ROWS // chunks
    for d in range(chunks):
        out_ref[d, :rows] = sums_ref[0, d * rows : (d + 1) * rows]
        tail = sums_ref[1, d * rows : (d + 1) * rows]
        out_ref[d, rows:] = tail[: rows // 2] + pltpu.roll(tail[rows // 2 :], lanes // 2, 1)


def gate_body(matrix_ref, parts_ref, out_ref):
    chunks, packed, lanes = parts_ref.shape
    rows = packed * 2 // 3
    cores = []
    for f in range(2):
        total = parts_ref[f]
        for d in range(f + 2, chunks, 2):
            total += parts_ref[d]
        tail = total[rows:]
        tail = jnp.concatenate([tail[:, : lanes // 2], tail[:, lanes // 2 :]], 0)
        cores.append(jnp.concatenate([total[:rows], tail], 1))
    gated = jnp.dot(
        matrix_ref[...], jnp.concatenate(cores, 0), precision=HIGHEST, preferred_element_type=F32
    ).astype(BF16)
    for f in range(2):
        mine = gated[f * rows : (f + 1) * rows]
        tail = mine[:, lanes:]
        tail = jnp.concatenate([tail[: rows // 2], tail[rows // 2 :]], 1)
        mine = jnp.concatenate([mine[:, :lanes], tail], 0)
        for d in range(f, chunks, 2):
            out_ref[d] = mine


def adjoint_body(win_ref, resp_ref, out_ref, wide_ref, sums_ref):
    chunks, packed, lanes = win_ref.shape
    rows = packed * 2 // 3
    points = chunks * rows // ROWS
    sources = resp_ref.shape[2]
    blocks = sums_ref.shape[0]
    for d in range(chunks):
        wide_ref[0, d * rows : (d + 1) * rows] = win_ref[d, :rows].astype(F32)
        tail = win_ref[d, rows:].astype(F32)
        half = d * rows + rows // 2
        wide_ref[1, d * rows : half] = tail
        wide_ref[1, half : (d + 1) * rows] = pltpu.roll(tail, lanes // 2, 1)

    def pick(row):
        pieces = [wide_ref[j, pl.ds(row, points, stride=ROWS), :] for j in range(2)]
        return jnp.concatenate(pieces, 1)[:, :sources]

    for k in range(HALF):
        real, imag = pick(k), pick(HALF + k)
        first = jnp.concatenate([real, imag], 0).astype(BF16)
        second = jnp.concatenate([imag, -real], 0).astype(BF16)
        sums = jnp.dot(first, resp_ref[0, k], preferred_element_type=F32)
        sums += jnp.dot(second, resp_ref[1, k], preferred_element_type=F32)
        for part in range(2):
            at = pl.ds(part * HALF + k, points, stride=ROWS)
            for j in range(blocks):
                sums_ref[j, at, :] = sums[
                    part * points : (part + 1) * points, j * lanes : (j + 1) * lanes
                ]
    for j in range(blocks):
        out_ref[:, j * lanes : (j + 1) * lanes] = sums_ref[j].astype(BF16)


def sum_body(got_ref, out_ref):
    total = got_ref[0].astype(F32)
    for d in range(1, got_ref.shape[0]):
        total += got_ref[d].astype(F32)
    out_ref[...] = total.astype(out_ref.dtype)


def focused_body(table_ref, sums_ref, out_ref, held_ref, sem_ref):
    steps, focal, cols = out_ref.shape
    high, middle, low = thirds(sums_ref[...])
    right = jnp.concatenate([high, middle, high, low, high, middle], 0)
    dims = (((0,), (0,)), ((), ()))
    pieces = sem_ref.shape[0]
    block = steps // pieces
    copies = []
    for i in range(pieces):
        left = table_ref[:, i * block * focal : (i + 1) * block * focal]
        values = lax.dot_general(left, right, dims, preferred_element_type=F32)
        at = pl.ds(i * block, block)
        held_ref[at] = values.astype(BF16).reshape(block, focal, cols)
        copies.append(pltpu.make_async_copy(held_ref.at[at], out_ref.at[at], sem_ref.at[i]))
        copies[-1].start()
    for copy in copies:
        copy.wait()


def focal_table(core_ids, core, steps, focal, scale):
    shape = (2 * focal * ROWS, steps * focal)
    row, col = iota(shape, 0), iota(shape, 1)
    held = jnp.where(row < focal * ROWS, core_ids[0], core_ids[1])
    table = wave(held * HALF + row % HALF, row // HALF % 2, core * steps + col // focal)
    return jnp.where(row // ROWS % focal == col % focal, table * scale, 0.0)


def shards(f_time, reflect, band_map, gates):
    steps, focal_here, cols = f_time.shape
    sources = reflect.shape[2]
    zh, zl, xl = (lax.axis_size(a) for a in SRC)
    pairs = zl * xl
    n_rcv = lax.axis_size(RCV)
    chunks = 2 * n_rcv
    focal = zh * pairs * focal_here
    core = lax.axis_index("c")
    own_rows = focal_here * ROWS
    struct = jax.ShapeDtypeStruct

    own, other, table = pl.pallas_call(
        spectra_body,
        out_shape=[struct((own_rows, cols), F32)] * 2
        + [struct((6 * 2 * own_rows, steps * focal_here), BF16)],
        in_specs=[pl.BlockSpec(memory_space=pltpu.HBM)],
        scratch_shapes=[pltpu.VMEM(f_time.shape, BF16), pltpu.SemaphoreType.DMA((4,))],
        compiler_params=pltpu.CompilerParams(vmem_limit_bytes=54784 << 10),
    )(f_time)
    others = lax.all_gather(other, "c", axis=0)
    others, core, gates, band_map = lax.optimization_barrier((others, core, gates, band_map))
    near = pl.pallas_call(
        near_body,
        out_shape=struct((zh, own_rows, cols), BF16),
        in_specs=[pl.BlockSpec(memory_space=pltpu.VMEM)] * 2,
        out_specs=pl.BlockSpec(memory_space=pltpu.HBM),
        scratch_shapes=[pltpu.VMEM((own_rows, cols), BF16), pltpu.SemaphoreType.DMA((zh,))],
        compiler_params=pltpu.CompilerParams(vmem_limit_bytes=12 << 20),
    )(own, others)
    near = far_all_to_all(near).reshape(zh * own_rows, cols)

    masked = vmem_call(
        masked_body,
        struct(reflect.shape, BF16),
        cost=pl.CostEstimate(flops=reflect.size, transcendentals=0, bytes_accessed=4 * reflect.size),
    )(band_map, reflect)

    part_rows = focal * ROWS // chunks
    part_focal = part_rows // ROWS
    shape = (2 * part_rows, NT)
    row, col = iota(shape, 0), iota(shape, 1)
    waves = wave(row // part_rows * HALF + row % HALF, row // HALF % 2, col)
    point = (lax.axis_index(RCV) * 2 + core) * part_focal + iota((2 * part_rows, focal), 0) // ROWS % part_focal
    block = point // focal_here
    far = block % zh * far_order(zh)[1] % zh
    point = (far * pairs + block // zh) * focal_here + point % focal_here
    window = jnp.where(point == iota((2 * part_rows, focal), 1), gates[None, :], 0).sum(1)
    inner = jnp.where(col < window[:, None], waves / math.sqrt(NT), 0.0)
    matrix = lax.dot_general(
        inner, waves * (2.0 / math.sqrt(NT)), (((1,), (1,)), ((), ())), precision=HIGHEST
    )
    shape = matrix.shape
    same = iota(shape, 0) // ROWS % part_focal == iota(shape, 1) // ROWS % part_focal
    matrix = jnp.where(same, matrix, 0.0)
    near, masked, matrix = lax.optimization_barrier((near, masked, matrix))
    every = jnp.broadcast_to(near[None], (pairs, zh * own_rows, cols))
    every = lax.all_to_all(every, PAIR, 0, 0, tiled=True).reshape(focal * ROWS, cols)

    packed = part_rows * 3 // 2
    parts = vmem_call(
        forward_body,
        struct((chunks, packed, LANES), F32),
        [
            pltpu.VMEM((cols // LANES, focal * ROWS, LANES), F32),
            pltpu.VMEM((2, focal * ROWS, LANES), F32),
        ],
    )(every, masked)
    parts = lax.all_to_all(parts, RCV + ("c",), 0, 0, tiled=True)

    gated = vmem_call(gate_body, struct((chunks, packed, LANES), BF16))(matrix, parts)
    windowed = lax.all_to_all(gated, RCV + ("c",), 0, 0, tiled=True)

    sends = vmem_call(
        adjoint_body,
        struct((focal * ROWS, cols), BF16),
        [
            pltpu.VMEM((2, focal * ROWS, LANES), F32),
            pltpu.VMEM((cols // LANES, focal * ROWS, LANES), F32),
        ],
    )(windowed, masked)
    got = lax.all_to_all(sends.reshape(pairs, zh * own_rows, cols), PAIR, 0, 0, tiled=True)
    got = vmem_call(sum_body, struct((zh * own_rows, cols), BF16))(got)
    got = far_all_to_all(got.reshape(zh, own_rows, cols))
    got = vmem_call(sum_body, struct((own_rows, cols), F32))(got)
    both = lax.all_gather(got, "c", axis=0, tiled=True)

    return pl.pallas_call(
        focused_body,
        out_shape=struct((steps, focal_here, cols), BF16),
        in_specs=[pl.BlockSpec(memory_space=pltpu.VMEM)] * 2,
        out_specs=pl.BlockSpec(memory_space=pltpu.HBM),
        scratch_shapes=[pltpu.VMEM(f_time.shape, BF16), pltpu.SemaphoreType.DMA((4,))],
        compiler_params=pltpu.CompilerParams(vmem_limit_bytes=12 << 20),
    )(table, both)


def solution(mesh):
    src, rcv, frq = (mesh.shape[a] for a in ("src", "rcv", "frq"))
    devices = mesh.devices.reshape(src // 4, 2, 2, rcv // 2, 2, frq)
    return jax.shard_map(
        shards,
        mesh=Mesh(devices, SRC + RCV + ("c",)),
        in_specs=(P("c", SRC, RCV), P(None, "c", SRC, RCV), P(SRC, RCV), P()),
        out_specs=P("c", SRC, RCV),
        check_vma=False,
    )
```

```python
import math

import jax
import jax.numpy as jnp
from jax import lax
from jax.experimental import pallas as pl
from jax.experimental.pallas import tpu as pltpu
from jax.sharding import Mesh, PartitionSpec as P

NT = 512
FREQ = 8
HALF = FREQ // 2
LANES = 128
HIGHEST = lax.Precision.HIGHEST
BF16 = jnp.bfloat16
F32 = jnp.float32
SRC = ("zh", "zl", "xl")
RCV = ("y", "xh")
PAIR = ("zl", "xl")
ROWS = 2 * HALF


def iota(shape, axis):
    return lax.broadcasted_iota(jnp.int32, shape, axis)


def wave(freq_ids, parts, sample_ids):
    phase = ((1 + freq_ids * NT // (2 * FREQ)) * sample_ids + parts * (NT // 4)) % NT
    return jnp.cos(phase.astype(F32) * (2.0 * math.pi / NT))


def thirds(x):
    high = x.astype(BF16)
    rest = x - high.astype(F32)
    middle = rest.astype(BF16)
    return high, middle, (rest - middle.astype(F32)).astype(BF16)


def vmem_call(body, out_shape, scratch=(), cost=None):
    return pl.pallas_call(
        body,
        out_shape=out_shape,
        scratch_shapes=list(scratch),
        cost_estimate=cost,
        compiler_params=pltpu.CompilerParams(vmem_limit_bytes=12 << 20),
    )


def far_order(count):
    order = list(range(count))
    if count % 2 or count < 4:
        return order
    half = far_order(count // 2)
    return [2 * j for j in half] + [2 * j + 1 for j in half]


def far_all_to_all(x):
    axes = SRC + RCV + ("c",)
    zh, *rest = (lax.axis_size(a) for a in axes)
    apart = math.prod(rest)
    groups = [[j * apart + i for j in far_order(zh)] for i in range(apart)]
    return lax.all_to_all(x, axes, 0, 0, tiled=True, axis_index_groups=groups)


def spectra_body(f_ref, own_ref, other_ref, last_ref, held_ref, sem_ref):
    steps, focal, cols = f_ref.shape
    pieces = sem_ref.shape[0]
    block = steps // pieces
    copies = []
    for i in range(pieces):
        at = pl.ds(i * block, block)
        copies.append(pltpu.make_async_copy(f_ref.at[at], held_ref.at[at], sem_ref.at[i]))
        copies[-1].start()
    core = lax.axis_index("c")
    table = focal_table((core, 1 - core), core, steps, focal, 1.0 / math.sqrt(NT))
    rows = table.shape[0]
    table = jnp.concatenate(thirds(table), 0)
    high, middle, low = thirds(focal_table((0, 1), core, steps, focal, 1.0 / math.sqrt(FREQ)))
    last_ref[...] = jnp.concatenate([high, high, middle, high, low, middle], 0)
    sums = 0.0
    for i, copy in enumerate(copies):
        copy.wait()
        merged = held_ref[i * block : (i + 1) * block].reshape(block * focal, cols)
        left = table[:, i * block * focal : (i + 1) * block * focal]
        sums += jnp.dot(left, merged, preferred_element_type=F32)
    sums = sums[:rows] + sums[rows : 2 * rows] + sums[2 * rows :]
    own_ref[...] = sums[: rows // 2]
    other_ref[...] = sums[rows // 2 :]


def near_body(own_ref, others_ref, out_ref, held_ref, sem_ref):
    core = lax.axis_index("c")
    held_ref[...] = (own_ref[...] + others_ref[1 - core]).astype(BF16)
    copies = []
    for j in range(out_ref.shape[0]):
        copies.append(pltpu.make_async_copy(held_ref, out_ref.at[j], sem_ref.at[j]))
        copies[-1].start()
    for copy in copies:
        copy.wait()


def masked_body(band_ref, resp_ref, out_ref):
    band = band_ref[...].astype(F32).astype(BF16)
    down, across = band.shape
    parts, _, sources, cols = resp_ref.shape
    shape = (across, cols)
    picks = (iota(shape, 0) == iota(shape, 1) // (cols // across)).astype(F32).astype(BF16)
    wide = jnp.dot(band, picks, preferred_element_type=F32).astype(BF16)
    shape = (sources, down)
    picks = (iota(shape, 0) // (sources // down) == iota(shape, 1)).astype(F32).astype(BF16)
    mask = jnp.dot(picks, wide, preferred_element_type=F32).astype(BF16)
    for c in range(parts):
        for k in range(HALF):
            out_ref[c, k] = resp_ref[c, k] * mask


def forward_body(spec_ref, resp_ref, out_ref, wide_ref, sums_ref):
    blocks = wide_ref.shape[0]
    points = spec_ref.shape[0] // ROWS
    chunks, _, lanes = out_ref.shape
    for j in range(blocks):
        wide_ref[j] = spec_ref[:, j * lanes : (j + 1) * lanes].astype(F32)

    def pick(row):
        pieces = [wide_ref[j, pl.ds(row, points, stride=ROWS), :] for j in range(blocks)]
        return jnp.concatenate(pieces, 1)

    for k in range(HALF):
        real, imag = pick(k), pick(HALF + k)
        first = jnp.concatenate([real, imag], 0).astype(BF16)
        second = jnp.concatenate([-imag, real], 0).astype(BF16)
        dims = (((1,), (1,)), ((), ()))
        sums = lax.dot_general(first, resp_ref[0, k], dims, preferred_element_type=F32)
        sums += lax.dot_general(second, resp_ref[1, k], dims, preferred_element_type=F32)
        head = sums[:, :lanes]
        rest = sums[:, lanes:]
        tail = jnp.concatenate(
            [rest, jnp.zeros((rest.shape[0], lanes - rest.shape[1]), F32)], 1
        )
        for part in range(2):
            at = pl.ds(part * HALF + k, points, stride=ROWS)
            sums_ref[0, at, :] = head[part * points : (part + 1) * points]
            sums_ref[1, at, :] = tail[part * points : (part + 1) * points]
    rows = points * ROWS // chunks
    for d in range(chunks):
        out_ref[d, :rows] = sums_ref[0, d * rows : (d + 1) * rows]
        tail = sums_ref[1, d * rows : (d + 1) * rows]
        out_ref[d, rows:] = tail[: rows // 2] + pltpu.roll(tail[rows // 2 :], lanes // 2, 1)


def gate_body(matrix_ref, parts_ref, out_ref):
    chunks, packed, lanes = parts_ref.shape
    rows = packed * 2 // 3
    cores = []
    for f in range(2):
        total = parts_ref[f]
        for d in range(f + 2, chunks, 2):
            total += parts_ref[d]
        tail = total[rows:]
        tail = jnp.concatenate([tail[:, : lanes // 2], tail[:, lanes // 2 :]], 0)
        cores.append(jnp.concatenate([total[:rows], tail], 1))
    gated = jnp.dot(
        matrix_ref[...], jnp.concatenate(cores, 0), precision=HIGHEST, preferred_element_type=F32
    ).astype(BF16)
    for f in range(2):
        mine = gated[f * rows : (f + 1) * rows]
        tail = mine[:, lanes:]
        tail = jnp.concatenate([tail[: rows // 2], tail[rows // 2 :]], 1)
        mine = jnp.concatenate([mine[:, :lanes], tail], 0)
        for d in range(f, chunks, 2):
            out_ref[d] = mine


def adjoint_body(win_ref, resp_ref, out_ref, wide_ref, sums_ref):
    chunks, packed, lanes = win_ref.shape
    rows = packed * 2 // 3
    points = chunks * rows // ROWS
    sources = resp_ref.shape[2]
    blocks = sums_ref.shape[0]
    for d in range(chunks):
        wide_ref[0, d * rows : (d + 1) * rows] = win_ref[d, :rows].astype(F32)
        tail = win_ref[d, rows:].astype(F32)
        half = d * rows + rows // 2
        wide_ref[1, d * rows : half] = tail
        wide_ref[1, half : (d + 1) * rows] = pltpu.roll(tail, lanes // 2, 1)

    def pick(row):
        pieces = [wide_ref[j, pl.ds(row, points, stride=ROWS), :] for j in range(2)]
        return jnp.concatenate(pieces, 1)[:, :sources]

    for k in range(HALF):
        real, imag = pick(k), pick(HALF + k)
        first = jnp.concatenate([real, imag], 0).astype(BF16)
        second = jnp.concatenate([imag, -real], 0).astype(BF16)
        sums = jnp.dot(first, resp_ref[0, k], preferred_element_type=F32)
        sums += jnp.dot(second, resp_ref[1, k], preferred_element_type=F32)
        for part in range(2):
            at = pl.ds(part * HALF + k, points, stride=ROWS)
            for j in range(blocks):
                sums_ref[j, at, :] = sums[
                    part * points : (part + 1) * points, j * lanes : (j + 1) * lanes
                ]
    for j in range(blocks):
        out_ref[:, j * lanes : (j + 1) * lanes] = sums_ref[j].astype(BF16)


def sum_body(got_ref, out_ref):
    total = got_ref[0].astype(F32)
    for d in range(1, got_ref.shape[0]):
        total += got_ref[d].astype(F32)
    out_ref[...] = total.astype(out_ref.dtype)


def focused_body(table_ref, sums_ref, out_ref, held_ref, sem_ref):
    steps, focal, cols = out_ref.shape
    high, middle, low = thirds(sums_ref[...])
    right = jnp.concatenate([high, middle, high, low, high, middle], 0)
    dims = (((0,), (0,)), ((), ()))
    pieces = sem_ref.shape[0]
    block = steps // pieces
    copies = []
    for i in range(pieces):
        left = table_ref[:, i * block * focal : (i + 1) * block * focal]
        values = lax.dot_general(left, right, dims, preferred_element_type=F32)
        at = pl.ds(i * block, block)
        held_ref[at] = values.astype(BF16).reshape(block, focal, cols)
        copies.append(pltpu.make_async_copy(held_ref.at[at], out_ref.at[at], sem_ref.at[i]))
        copies[-1].start()
    for copy in copies:
        copy.wait()


def focal_table(core_ids, core, steps, focal, scale):
    shape = (2 * focal * ROWS, steps * focal)
    row, col = iota(shape, 0), iota(shape, 1)
    held = jnp.where(row < focal * ROWS, core_ids[0], core_ids[1])
    table = wave(held * HALF + row % HALF, row // HALF % 2, core * steps + col // focal)
    return jnp.where(row // ROWS % focal == col % focal, table * scale, 0.0)


def shards(f_time, reflect, band_map, gates):
    steps, focal_here, cols = f_time.shape
    sources = reflect.shape[2]
    zh, zl, xl = (lax.axis_size(a) for a in SRC)
    pairs = zl * xl
    n_rcv = lax.axis_size(RCV)
    chunks = 2 * n_rcv
    focal = zh * pairs * focal_here
    core = lax.axis_index("c")
    own_rows = focal_here * ROWS
    struct = jax.ShapeDtypeStruct

    own, other, table = pl.pallas_call(
        spectra_body,
        out_shape=[struct((own_rows, cols), F32)] * 2
        + [struct((6 * 2 * own_rows, steps * focal_here), BF16)],
        in_specs=[pl.BlockSpec(memory_space=pltpu.HBM)],
        scratch_shapes=[pltpu.VMEM(f_time.shape, BF16), pltpu.SemaphoreType.DMA((4,))],
        compiler_params=pltpu.CompilerParams(vmem_limit_bytes=54784 << 10),
    )(f_time)
    others = lax.all_gather(other, "c", axis=0)
    others, core, gates, band_map = lax.optimization_barrier((others, core, gates, band_map))
    near = pl.pallas_call(
        near_body,
        out_shape=struct((zh, own_rows, cols), BF16),
        in_specs=[pl.BlockSpec(memory_space=pltpu.VMEM)] * 2,
        out_specs=pl.BlockSpec(memory_space=pltpu.HBM),
        scratch_shapes=[pltpu.VMEM((own_rows, cols), BF16), pltpu.SemaphoreType.DMA((zh,))],
        compiler_params=pltpu.CompilerParams(vmem_limit_bytes=12 << 20),
    )(own, others)
    near = far_all_to_all(near).reshape(zh * own_rows, cols)

    masked = vmem_call(
        masked_body,
        struct(reflect.shape, BF16),
        cost=pl.CostEstimate(flops=reflect.size, transcendentals=0, bytes_accessed=4 * reflect.size),
    )(band_map, reflect)

    part_rows = focal * ROWS // chunks
    part_focal = part_rows // ROWS
    shape = (2 * part_rows, NT)
    row, col = iota(shape, 0), iota(shape, 1)
    waves = wave(row // part_rows * HALF + row % HALF, row // HALF % 2, col)
    point = (lax.axis_index(RCV) * 2 + core) * part_focal + iota((2 * part_rows, focal), 0) // ROWS % part_focal
    block = point // focal_here
    far = sum(jnp.where(block % zh == j, f, 0) for j, f in enumerate(far_order(zh)))
    point = (far * pairs + block // zh) * focal_here + point % focal_here
    window = jnp.where(point == iota((2 * part_rows, focal), 1), gates[None, :], 0).sum(1)
    inner = jnp.where(col < window[:, None], waves / math.sqrt(NT), 0.0)
    matrix = lax.dot_general(
        inner, waves * (2.0 / math.sqrt(NT)), (((1,), (1,)), ((), ())), precision=HIGHEST
    )
    shape = matrix.shape
    same = iota(shape, 0) // ROWS % part_focal == iota(shape, 1) // ROWS % part_focal
    matrix = jnp.where(same, matrix, 0.0)
    near, masked, matrix = lax.optimization_barrier((near, masked, matrix))
    every = jnp.broadcast_to(near[None], (pairs, zh * own_rows, cols))
    every = lax.all_to_all(every, PAIR, 0, 0, tiled=True).reshape(focal * ROWS, cols)

    packed = part_rows * 3 // 2
    parts = vmem_call(
        forward_body,
        struct((chunks, packed, LANES), F32),
        [
            pltpu.VMEM((cols // LANES, focal * ROWS, LANES), F32),
            pltpu.VMEM((2, focal * ROWS, LANES), F32),
        ],
    )(every, masked)
    parts = lax.all_to_all(parts, RCV + ("c",), 0, 0, tiled=True)

    gated = vmem_call(gate_body, struct((chunks, packed, LANES), BF16))(matrix, parts)
    windowed = lax.all_to_all(gated, RCV + ("c",), 0, 0, tiled=True)

    sends = vmem_call(
        adjoint_body,
        struct((focal * ROWS, cols), BF16),
        [
            pltpu.VMEM((2, focal * ROWS, LANES), F32),
            pltpu.VMEM((cols // LANES, focal * ROWS, LANES), F32),
        ],
    )(windowed, masked)
    got = lax.all_to_all(sends.reshape(pairs, zh * own_rows, cols), PAIR, 0, 0, tiled=True)
    got = vmem_call(sum_body, struct((zh * own_rows, cols), BF16))(got)
    got = far_all_to_all(got.reshape(zh, own_rows, cols))
    got = vmem_call(sum_body, struct((own_rows, cols), F32))(got)
    both = lax.all_gather(got, "c", axis=0, tiled=True)

    return pl.pallas_call(
        focused_body,
        out_shape=struct((steps, focal_here, cols), BF16),
        in_specs=[pl.BlockSpec(memory_space=pltpu.VMEM)] * 2,
        out_specs=pl.BlockSpec(memory_space=pltpu.HBM),
        scratch_shapes=[pltpu.VMEM(f_time.shape, BF16), pltpu.SemaphoreType.DMA((4,))],
        compiler_params=pltpu.CompilerParams(vmem_limit_bytes=12 << 20),
    )(table, both)


def solution(mesh):
    src, rcv, frq = (mesh.shape[a] for a in ("src", "rcv", "frq"))
    devices = mesh.devices.reshape(src // 4, 2, 2, rcv // 2, 2, frq)
    return jax.shard_map(
        shards,
        mesh=Mesh(devices, SRC + RCV + ("c",)),
        in_specs=(P("c", SRC, RCV), P(None, "c", SRC, RCV), P(SRC, RCV), P()),
        out_specs=P("c", SRC, RCV),
        check_vma=False,
    )
```

```python
import math

import jax
import jax.numpy as jnp
from jax import lax
from jax.experimental import pallas as pl
from jax.experimental.pallas import tpu as pltpu
from jax.sharding import Mesh, PartitionSpec as P

NT = 512
FREQ = 8
HALF = FREQ // 2
LANES = 128
HIGHEST = lax.Precision.HIGHEST
BF16 = jnp.bfloat16
F32 = jnp.float32
SRC = ("zh", "zl", "xl")
RCV = ("y", "xh")
PAIR = ("zl", "xl")
ROWS = 2 * HALF


def iota(shape, axis):
    return lax.broadcasted_iota(jnp.int32, shape, axis)


def wave(freq_ids, parts, sample_ids):
    phase = ((1 + freq_ids * NT // (2 * FREQ)) * sample_ids + parts * (NT // 4)) % NT
    return jnp.cos(phase.astype(F32) * (2.0 * math.pi / NT))


def thirds(x):
    high = x.astype(BF16)
    rest = x - high.astype(F32)
    middle = rest.astype(BF16)
    return high, middle, (rest - middle.astype(F32)).astype(BF16)


def vmem_call(body, out_shape, scratch=(), cost=None):
    return pl.pallas_call(
        body,
        out_shape=out_shape,
        scratch_shapes=list(scratch),
        cost_estimate=cost,
        compiler_params=pltpu.CompilerParams(vmem_limit_bytes=12 << 20),
    )


def far_order(count):
    half = count // 2
    order = [j for i in range(half) for j in (i, i + half)]
    return order + list(range(2 * half, count))


def far_all_to_all(x):
    axes = SRC + RCV + ("c",)
    zh, *rest = (lax.axis_size(a) for a in axes)
    apart = math.prod(rest)
    groups = [[j * apart + i for j in far_order(zh)] for i in range(apart)]
    return lax.all_to_all(x, axes, 0, 0, tiled=True, axis_index_groups=groups)


def spectra_body(f_ref, own_ref, other_ref, last_ref, held_ref, sem_ref):
    steps, focal, cols = f_ref.shape
    pieces = sem_ref.shape[0]
    block = steps // pieces
    copies = []
    for i in range(pieces):
        at = pl.ds(i * block, block)
        copies.append(pltpu.make_async_copy(f_ref.at[at], held_ref.at[at], sem_ref.at[i]))
        copies[-1].start()
    core = lax.axis_index("c")
    table = focal_table((core, 1 - core), core, steps, focal, 1.0 / math.sqrt(NT))
    rows = table.shape[0]
    table = jnp.concatenate(thirds(table), 0)
    high, middle, low = thirds(focal_table((0, 1), core, steps, focal, 1.0 / math.sqrt(FREQ)))
    last_ref[...] = jnp.concatenate([high, high, middle, high, low, middle], 0)
    sums = 0.0
    for i, copy in enumerate(copies):
        copy.wait()
        merged = held_ref[i * block : (i + 1) * block].reshape(block * focal, cols)
        left = table[:, i * block * focal : (i + 1) * block * focal]
        sums += jnp.dot(left, merged, preferred_element_type=F32)
    sums = sums[:rows] + sums[rows : 2 * rows] + sums[2 * rows :]
    own_ref[...] = sums[: rows // 2]
    other_ref[...] = sums[rows // 2 :]


def near_body(own_ref, others_ref, out_ref, held_ref, sem_ref):
    core = lax.axis_index("c")
    held_ref[...] = (own_ref[...] + others_ref[1 - core]).astype(BF16)
    copies = []
    for j in range(out_ref.shape[0]):
        copies.append(pltpu.make_async_copy(held_ref, out_ref.at[j], sem_ref.at[j]))
        copies[-1].start()
    for copy in copies:
        copy.wait()


def masked_body(band_ref, resp_ref, out_ref):
    band = band_ref[...].astype(F32).astype(BF16)
    down, across = band.shape
    parts, _, sources, cols = resp_ref.shape
    shape = (across, cols)
    picks = (iota(shape, 0) == iota(shape, 1) // (cols // across)).astype(F32).astype(BF16)
    wide = jnp.dot(band, picks, preferred_element_type=F32).astype(BF16)
    shape = (sources, down)
    picks = (iota(shape, 0) // (sources // down) == iota(shape, 1)).astype(F32).astype(BF16)
    mask = jnp.dot(picks, wide, preferred_element_type=F32).astype(BF16)
    for c in range(parts):
        for k in range(HALF):
            out_ref[c, k] = resp_ref[c, k] * mask


def forward_body(spec_ref, resp_ref, out_ref, wide_ref, sums_ref):
    blocks = wide_ref.shape[0]
    points = spec_ref.shape[0] // ROWS
    chunks, _, lanes = out_ref.shape
    for j in range(blocks):
        wide_ref[j] = spec_ref[:, j * lanes : (j + 1) * lanes].astype(F32)

    def pick(row):
        pieces = [wide_ref[j, pl.ds(row, points, stride=ROWS), :] for j in range(blocks)]
        return jnp.concatenate(pieces, 1)

    for k in range(HALF):
        real, imag = pick(k), pick(HALF + k)
        first = jnp.concatenate([real, imag], 0).astype(BF16)
        second = jnp.concatenate([-imag, real], 0).astype(BF16)
        dims = (((1,), (1,)), ((), ()))
        sums = lax.dot_general(first, resp_ref[0, k], dims, preferred_element_type=F32)
        sums += lax.dot_general(second, resp_ref[1, k], dims, preferred_element_type=F32)
        head = sums[:, :lanes]
        rest = sums[:, lanes:]
        tail = jnp.concatenate(
            [rest, jnp.zeros((rest.shape[0], lanes - rest.shape[1]), F32)], 1
        )
        for part in range(2):
            at = pl.ds(part * HALF + k, points, stride=ROWS)
            sums_ref[0, at, :] = head[part * points : (part + 1) * points]
            sums_ref[1, at, :] = tail[part * points : (part + 1) * points]
    rows = points * ROWS // chunks
    for d in range(chunks):
        out_ref[d, :rows] = sums_ref[0, d * rows : (d + 1) * rows]
        tail = sums_ref[1, d * rows : (d + 1) * rows]
        out_ref[d, rows:] = tail[: rows // 2] + pltpu.roll(tail[rows // 2 :], lanes // 2, 1)


def gate_body(matrix_ref, parts_ref, out_ref):
    chunks, packed, lanes = parts_ref.shape
    rows = packed * 2 // 3
    cores = []
    for f in range(2):
        total = parts_ref[f]
        for d in range(f + 2, chunks, 2):
            total += parts_ref[d]
        tail = total[rows:]
        tail = jnp.concatenate([tail[:, : lanes // 2], tail[:, lanes // 2 :]], 0)
        cores.append(jnp.concatenate([total[:rows], tail], 1))
    gated = jnp.dot(
        matrix_ref[...], jnp.concatenate(cores, 0), precision=HIGHEST, preferred_element_type=F32
    ).astype(BF16)
    for f in range(2):
        mine = gated[f * rows : (f + 1) * rows]
        tail = mine[:, lanes:]
        tail = jnp.concatenate([tail[: rows // 2], tail[rows // 2 :]], 1)
        mine = jnp.concatenate([mine[:, :lanes], tail], 0)
        for d in range(f, chunks, 2):
            out_ref[d] = mine


def adjoint_body(win_ref, resp_ref, out_ref, wide_ref, sums_ref):
    chunks, packed, lanes = win_ref.shape
    rows = packed * 2 // 3
    points = chunks * rows // ROWS
    sources = resp_ref.shape[2]
    blocks = sums_ref.shape[0]
    for d in range(chunks):
        wide_ref[0, d * rows : (d + 1) * rows] = win_ref[d, :rows].astype(F32)
        tail = win_ref[d, rows:].astype(F32)
        half = d * rows + rows // 2
        wide_ref[1, d * rows : half] = tail
        wide_ref[1, half : (d + 1) * rows] = pltpu.roll(tail, lanes // 2, 1)

    def pick(row):
        pieces = [wide_ref[j, pl.ds(row, points, stride=ROWS), :] for j in range(2)]
        return jnp.concatenate(pieces, 1)[:, :sources]

    for k in range(HALF):
        real, imag = pick(k), pick(HALF + k)
        first = jnp.concatenate([real, imag], 0).astype(BF16)
        second = jnp.concatenate([imag, -real], 0).astype(BF16)
        sums = jnp.dot(first, resp_ref[0, k], preferred_element_type=F32)
        sums += jnp.dot(second, resp_ref[1, k], preferred_element_type=F32)
        for part in range(2):
            at = pl.ds(part * HALF + k, points, stride=ROWS)
            for j in range(blocks):
                sums_ref[j, at, :] = sums[
                    part * points : (part + 1) * points, j * lanes : (j + 1) * lanes
                ]
    for j in range(blocks):
        out_ref[:, j * lanes : (j + 1) * lanes] = sums_ref[j].astype(BF16)


def sum_body(got_ref, out_ref):
    total = got_ref[0].astype(F32)
    for d in range(1, got_ref.shape[0]):
        total += got_ref[d].astype(F32)
    out_ref[...] = total.astype(out_ref.dtype)


def focused_body(table_ref, sums_ref, out_ref, held_ref, sem_ref):
    steps, focal, cols = out_ref.shape
    high, middle, low = thirds(sums_ref[...])
    right = jnp.concatenate([high, middle, high, low, high, middle], 0)
    dims = (((0,), (0,)), ((), ()))
    pieces = sem_ref.shape[0]
    block = steps // pieces
    copies = []
    for i in range(pieces):
        left = table_ref[:, i * block * focal : (i + 1) * block * focal]
        values = lax.dot_general(left, right, dims, preferred_element_type=F32)
        at = pl.ds(i * block, block)
        held_ref[at] = values.astype(BF16).reshape(block, focal, cols)
        copies.append(pltpu.make_async_copy(held_ref.at[at], out_ref.at[at], sem_ref.at[i]))
        copies[-1].start()
    for copy in copies:
        copy.wait()


def focal_table(core_ids, core, steps, focal, scale):
    shape = (2 * focal * ROWS, steps * focal)
    row, col = iota(shape, 0), iota(shape, 1)
    held = jnp.where(row < focal * ROWS, core_ids[0], core_ids[1])
    table = wave(held * HALF + row % HALF, row // HALF % 2, core * steps + col // focal)
    return jnp.where(row // ROWS % focal == col % focal, table * scale, 0.0)


def shards(f_time, reflect, band_map, gates):
    steps, focal_here, cols = f_time.shape
    sources = reflect.shape[2]
    zh, zl, xl = (lax.axis_size(a) for a in SRC)
    pairs = zl * xl
    n_rcv = lax.axis_size(RCV)
    chunks = 2 * n_rcv
    focal = zh * pairs * focal_here
    core = lax.axis_index("c")
    own_rows = focal_here * ROWS
    struct = jax.ShapeDtypeStruct

    own, other, table = pl.pallas_call(
        spectra_body,
        out_shape=[struct((own_rows, cols), F32)] * 2
        + [struct((6 * 2 * own_rows, steps * focal_here), BF16)],
        in_specs=[pl.BlockSpec(memory_space=pltpu.HBM)],
        scratch_shapes=[pltpu.VMEM(f_time.shape, BF16), pltpu.SemaphoreType.DMA((4,))],
        compiler_params=pltpu.CompilerParams(vmem_limit_bytes=54784 << 10),
    )(f_time)
    others = lax.all_gather(other, "c", axis=0)
    others, core, gates, band_map = lax.optimization_barrier((others, core, gates, band_map))
    near = pl.pallas_call(
        near_body,
        out_shape=struct((zh, own_rows, cols), BF16),
        in_specs=[pl.BlockSpec(memory_space=pltpu.VMEM)] * 2,
        out_specs=pl.BlockSpec(memory_space=pltpu.HBM),
        scratch_shapes=[pltpu.VMEM((own_rows, cols), BF16), pltpu.SemaphoreType.DMA((zh,))],
        compiler_params=pltpu.CompilerParams(vmem_limit_bytes=12 << 20),
    )(own, others)
    near = far_all_to_all(near).reshape(zh * own_rows, cols)

    masked = vmem_call(
        masked_body,
        struct(reflect.shape, BF16),
        cost=pl.CostEstimate(flops=reflect.size, transcendentals=0, bytes_accessed=4 * reflect.size),
    )(band_map, reflect)

    part_rows = focal * ROWS // chunks
    part_focal = part_rows // ROWS
    shape = (2 * part_rows, NT)
    row, col = iota(shape, 0), iota(shape, 1)
    waves = wave(row // part_rows * HALF + row % HALF, row // HALF % 2, col)
    point = (lax.axis_index(RCV) * 2 + core) * part_focal + iota((2 * part_rows, focal), 0) // ROWS % part_focal
    block = point // focal_here
    far = sum(jnp.where(block % zh == j, f, 0) for j, f in enumerate(far_order(zh)))
    point = (far * pairs + block // zh) * focal_here + point % focal_here
    window = jnp.where(point == iota((2 * part_rows, focal), 1), gates[None, :], 0).sum(1)
    inner = jnp.where(col < window[:, None], waves / math.sqrt(NT), 0.0)
    matrix = lax.dot_general(
        inner, waves * (2.0 / math.sqrt(NT)), (((1,), (1,)), ((), ())), precision=HIGHEST
    )
    shape = matrix.shape
    same = iota(shape, 0) // ROWS % part_focal == iota(shape, 1) // ROWS % part_focal
    matrix = jnp.where(same, matrix, 0.0)
    near, masked, matrix = lax.optimization_barrier((near, masked, matrix))
    every = jnp.broadcast_to(near[None], (pairs, zh * own_rows, cols))
    every = lax.all_to_all(every, PAIR, 0, 0, tiled=True).reshape(focal * ROWS, cols)

    packed = part_rows * 3 // 2
    parts = vmem_call(
        forward_body,
        struct((chunks, packed, LANES), F32),
        [
            pltpu.VMEM((cols // LANES, focal * ROWS, LANES), F32),
            pltpu.VMEM((2, focal * ROWS, LANES), F32),
        ],
    )(every, masked)
    parts = lax.all_to_all(parts, RCV + ("c",), 0, 0, tiled=True)

    gated = vmem_call(gate_body, struct((chunks, packed, LANES), BF16))(matrix, parts)
    windowed = lax.all_to_all(gated, RCV + ("c",), 0, 0, tiled=True)

    sends = vmem_call(
        adjoint_body,
        struct((focal * ROWS, cols), BF16),
        [
            pltpu.VMEM((2, focal * ROWS, LANES), F32),
            pltpu.VMEM((cols // LANES, focal * ROWS, LANES), F32),
        ],
    )(windowed, masked)
    got = lax.all_to_all(sends.reshape(pairs, zh * own_rows, cols), PAIR, 0, 0, tiled=True)
    got = vmem_call(sum_body, struct((zh * own_rows, cols), BF16))(got)
    got = far_all_to_all(got.reshape(zh, own_rows, cols))
    got = vmem_call(sum_body, struct((own_rows, cols), F32))(got)
    both = lax.all_gather(got, "c", axis=0, tiled=True)

    return pl.pallas_call(
        focused_body,
        out_shape=struct((steps, focal_here, cols), BF16),
        in_specs=[pl.BlockSpec(memory_space=pltpu.VMEM)] * 2,
        out_specs=pl.BlockSpec(memory_space=pltpu.HBM),
        scratch_shapes=[pltpu.VMEM(f_time.shape, BF16), pltpu.SemaphoreType.DMA((4,))],
        compiler_params=pltpu.CompilerParams(vmem_limit_bytes=12 << 20),
    )(table, both)


def solution(mesh):
    src, rcv, frq = (mesh.shape[a] for a in ("src", "rcv", "frq"))
    devices = mesh.devices.reshape(src // 4, 2, 2, rcv // 2, 2, frq)
    return jax.shard_map(
        shards,
        mesh=Mesh(devices, SRC + RCV + ("c",)),
        in_specs=(P("c", SRC, RCV), P(None, "c", SRC, RCV), P(SRC, RCV), P()),
        out_specs=P("c", SRC, RCV),
        check_vma=False,
    )
```

```python
import math

import jax
import jax.numpy as jnp
from jax import lax
from jax.experimental import pallas as pl
from jax.experimental.pallas import tpu as pltpu
from jax.sharding import Mesh, PartitionSpec as P

NT = 512
FREQ = 8
HALF = FREQ // 2
LANES = 128
HIGHEST = lax.Precision.HIGHEST
BF16 = jnp.bfloat16
F32 = jnp.float32
SRC = ("zh", "zl", "xl")
RCV = ("y", "xh")
PAIR = ("zl", "xl")
ROWS = 2 * HALF


def iota(shape, axis):
    return lax.broadcasted_iota(jnp.int32, shape, axis)


def wave(freq_ids, parts, sample_ids):
    phase = ((1 + freq_ids * NT // (2 * FREQ)) * sample_ids + parts * (NT // 4)) % NT
    return jnp.cos(phase.astype(F32) * (2.0 * math.pi / NT))


def thirds(x):
    high = x.astype(BF16)
    rest = x - high.astype(F32)
    middle = rest.astype(BF16)
    return high, middle, (rest - middle.astype(F32)).astype(BF16)


def vmem_call(body, out_shape, scratch=(), cost=None):
    return pl.pallas_call(
        body,
        out_shape=out_shape,
        scratch_shapes=list(scratch),
        cost_estimate=cost,
        compiler_params=pltpu.CompilerParams(vmem_limit_bytes=12 << 20),
    )


def far_order(count):
    order = list(range(count))
    if count % 2 or count < 4:
        return order
    half = far_order(count // 2)
    turn = half[len(half) // 2 :] + half[: len(half) // 2]
    return [2 * j for j in half] + [2 * j + 1 for j in turn]


def far_all_to_all(x):
    axes = SRC + RCV + ("c",)
    zh, *rest = (lax.axis_size(a) for a in axes)
    apart = math.prod(rest)
    groups = [[j * apart + i for j in far_order(zh)] for i in range(apart)]
    return lax.all_to_all(x, axes, 0, 0, tiled=True, axis_index_groups=groups)


def spectra_body(f_ref, own_ref, other_ref, last_ref, held_ref, sem_ref):
    steps, focal, cols = f_ref.shape
    pieces = sem_ref.shape[0]
    block = steps // pieces
    copies = []
    for i in range(pieces):
        at = pl.ds(i * block, block)
        copies.append(pltpu.make_async_copy(f_ref.at[at], held_ref.at[at], sem_ref.at[i]))
        copies[-1].start()
    core = lax.axis_index("c")
    table = focal_table((core, 1 - core), core, steps, focal, 1.0 / math.sqrt(NT))
    rows = table.shape[0]
    table = jnp.concatenate(thirds(table), 0)
    high, middle, low = thirds(focal_table((0, 1), core, steps, focal, 1.0 / math.sqrt(FREQ)))
    last_ref[...] = jnp.concatenate([high, high, middle, high, low, middle], 0)
    sums = 0.0
    for i, copy in enumerate(copies):
        copy.wait()
        merged = held_ref[i * block : (i + 1) * block].reshape(block * focal, cols)
        left = table[:, i * block * focal : (i + 1) * block * focal]
        sums += jnp.dot(left, merged, preferred_element_type=F32)
    sums = sums[:rows] + sums[rows : 2 * rows] + sums[2 * rows :]
    own_ref[...] = sums[: rows // 2]
    other_ref[...] = sums[rows // 2 :]


def near_body(own_ref, others_ref, out_ref, held_ref, sem_ref):
    core = lax.axis_index("c")
    held_ref[...] = (own_ref[...] + others_ref[1 - core]).astype(BF16)
    copies = []
    for j in range(out_ref.shape[0]):
        copies.append(pltpu.make_async_copy(held_ref, out_ref.at[j], sem_ref.at[j]))
        copies[-1].start()
    for copy in copies:
        copy.wait()


def masked_body(band_ref, resp_ref, out_ref):
    band = band_ref[...].astype(F32).astype(BF16)
    down, across = band.shape
    parts, _, sources, cols = resp_ref.shape
    shape = (across, cols)
    picks = (iota(shape, 0) == iota(shape, 1) // (cols // across)).astype(F32).astype(BF16)
    wide = jnp.dot(band, picks, preferred_element_type=F32).astype(BF16)
    shape = (sources, down)
    picks = (iota(shape, 0) // (sources // down) == iota(shape, 1)).astype(F32).astype(BF16)
    mask = jnp.dot(picks, wide, preferred_element_type=F32).astype(BF16)
    for c in range(parts):
        for k in range(HALF):
            out_ref[c, k] = resp_ref[c, k] * mask


def forward_body(spec_ref, resp_ref, out_ref, wide_ref, sums_ref):
    blocks = wide_ref.shape[0]
    points = spec_ref.shape[0] // ROWS
    chunks, _, lanes = out_ref.shape
    for j in range(blocks):
        wide_ref[j] = spec_ref[:, j * lanes : (j + 1) * lanes].astype(F32)

    def pick(row):
        pieces = [wide_ref[j, pl.ds(row, points, stride=ROWS), :] for j in range(blocks)]
        return jnp.concatenate(pieces, 1)

    for k in range(HALF):
        real, imag = pick(k), pick(HALF + k)
        first = jnp.concatenate([real, imag], 0).astype(BF16)
        second = jnp.concatenate([-imag, real], 0).astype(BF16)
        dims = (((1,), (1,)), ((), ()))
        sums = lax.dot_general(first, resp_ref[0, k], dims, preferred_element_type=F32)
        sums += lax.dot_general(second, resp_ref[1, k], dims, preferred_element_type=F32)
        head = sums[:, :lanes]
        rest = sums[:, lanes:]
        tail = jnp.concatenate(
            [rest, jnp.zeros((rest.shape[0], lanes - rest.shape[1]), F32)], 1
        )
        for part in range(2):
            at = pl.ds(part * HALF + k, points, stride=ROWS)
            sums_ref[0, at, :] = head[part * points : (part + 1) * points]
            sums_ref[1, at, :] = tail[part * points : (part + 1) * points]
    rows = points * ROWS // chunks
    for d in range(chunks):
        out_ref[d, :rows] = sums_ref[0, d * rows : (d + 1) * rows]
        tail = sums_ref[1, d * rows : (d + 1) * rows]
        out_ref[d, rows:] = tail[: rows // 2] + pltpu.roll(tail[rows // 2 :], lanes // 2, 1)


def gate_body(matrix_ref, parts_ref, out_ref):
    chunks, packed, lanes = parts_ref.shape
    rows = packed * 2 // 3
    cores = []
    for f in range(2):
        total = parts_ref[f]
        for d in range(f + 2, chunks, 2):
            total += parts_ref[d]
        tail = total[rows:]
        tail = jnp.concatenate([tail[:, : lanes // 2], tail[:, lanes // 2 :]], 0)
        cores.append(jnp.concatenate([total[:rows], tail], 1))
    gated = jnp.dot(
        matrix_ref[...], jnp.concatenate(cores, 0), precision=HIGHEST, preferred_element_type=F32
    ).astype(BF16)
    for f in range(2):
        mine = gated[f * rows : (f + 1) * rows]
        tail = mine[:, lanes:]
        tail = jnp.concatenate([tail[: rows // 2], tail[rows // 2 :]], 1)
        mine = jnp.concatenate([mine[:, :lanes], tail], 0)
        for d in range(f, chunks, 2):
            out_ref[d] = mine


def adjoint_body(win_ref, resp_ref, out_ref, wide_ref, sums_ref):
    chunks, packed, lanes = win_ref.shape
    rows = packed * 2 // 3
    points = chunks * rows // ROWS
    sources = resp_ref.shape[2]
    blocks = sums_ref.shape[0]
    for d in range(chunks):
        wide_ref[0, d * rows : (d + 1) * rows] = win_ref[d, :rows].astype(F32)
        tail = win_ref[d, rows:].astype(F32)
        half = d * rows + rows // 2
        wide_ref[1, d * rows : half] = tail
        wide_ref[1, half : (d + 1) * rows] = pltpu.roll(tail, lanes // 2, 1)

    def pick(row):
        pieces = [wide_ref[j, pl.ds(row, points, stride=ROWS), :] for j in range(2)]
        return jnp.concatenate(pieces, 1)[:, :sources]

    for k in range(HALF):
        real, imag = pick(k), pick(HALF + k)
        first = jnp.concatenate([real, imag], 0).astype(BF16)
        second = jnp.concatenate([imag, -real], 0).astype(BF16)
        sums = jnp.dot(first, resp_ref[0, k], preferred_element_type=F32)
        sums += jnp.dot(second, resp_ref[1, k], preferred_element_type=F32)
        for part in range(2):
            at = pl.ds(part * HALF + k, points, stride=ROWS)
            for j in range(blocks):
                sums_ref[j, at, :] = sums[
                    part * points : (part + 1) * points, j * lanes : (j + 1) * lanes
                ]
    for j in range(blocks):
        out_ref[:, j * lanes : (j + 1) * lanes] = sums_ref[j].astype(BF16)


def sum_body(got_ref, out_ref):
    total = got_ref[0].astype(F32)
    for d in range(1, got_ref.shape[0]):
        total += got_ref[d].astype(F32)
    out_ref[...] = total.astype(out_ref.dtype)


def focused_body(table_ref, sums_ref, out_ref, held_ref, sem_ref):
    steps, focal, cols = out_ref.shape
    high, middle, low = thirds(sums_ref[...])
    right = jnp.concatenate([high, middle, high, low, high, middle], 0)
    dims = (((0,), (0,)), ((), ()))
    pieces = sem_ref.shape[0]
    block = steps // pieces
    copies = []
    for i in range(pieces):
        left = table_ref[:, i * block * focal : (i + 1) * block * focal]
        values = lax.dot_general(left, right, dims, preferred_element_type=F32)
        at = pl.ds(i * block, block)
        held_ref[at] = values.astype(BF16).reshape(block, focal, cols)
        copies.append(pltpu.make_async_copy(held_ref.at[at], out_ref.at[at], sem_ref.at[i]))
        copies[-1].start()
    for copy in copies:
        copy.wait()


def focal_table(core_ids, core, steps, focal, scale):
    shape = (2 * focal * ROWS, steps * focal)
    row, col = iota(shape, 0), iota(shape, 1)
    held = jnp.where(row < focal * ROWS, core_ids[0], core_ids[1])
    table = wave(held * HALF + row % HALF, row // HALF % 2, core * steps + col // focal)
    return jnp.where(row // ROWS % focal == col % focal, table * scale, 0.0)


def shards(f_time, reflect, band_map, gates):
    steps, focal_here, cols = f_time.shape
    sources = reflect.shape[2]
    zh, zl, xl = (lax.axis_size(a) for a in SRC)
    pairs = zl * xl
    n_rcv = lax.axis_size(RCV)
    chunks = 2 * n_rcv
    focal = zh * pairs * focal_here
    core = lax.axis_index("c")
    own_rows = focal_here * ROWS
    struct = jax.ShapeDtypeStruct

    own, other, table = pl.pallas_call(
        spectra_body,
        out_shape=[struct((own_rows, cols), F32)] * 2
        + [struct((6 * 2 * own_rows, steps * focal_here), BF16)],
        in_specs=[pl.BlockSpec(memory_space=pltpu.HBM)],
        scratch_shapes=[pltpu.VMEM(f_time.shape, BF16), pltpu.SemaphoreType.DMA((4,))],
        compiler_params=pltpu.CompilerParams(vmem_limit_bytes=54784 << 10),
    )(f_time)
    others = lax.all_gather(other, "c", axis=0)
    others, core, gates, band_map = lax.optimization_barrier((others, core, gates, band_map))
    near = pl.pallas_call(
        near_body,
        out_shape=struct((zh, own_rows, cols), BF16),
        in_specs=[pl.BlockSpec(memory_space=pltpu.VMEM)] * 2,
        out_specs=pl.BlockSpec(memory_space=pltpu.HBM),
        scratch_shapes=[pltpu.VMEM((own_rows, cols), BF16), pltpu.SemaphoreType.DMA((zh,))],
        compiler_params=pltpu.CompilerParams(vmem_limit_bytes=12 << 20),
    )(own, others)
    near = far_all_to_all(near).reshape(zh * own_rows, cols)

    masked = vmem_call(
        masked_body,
        struct(reflect.shape, BF16),
        cost=pl.CostEstimate(flops=reflect.size, transcendentals=0, bytes_accessed=4 * reflect.size),
    )(band_map, reflect)

    part_rows = focal * ROWS // chunks
    part_focal = part_rows // ROWS
    shape = (2 * part_rows, NT)
    row, col = iota(shape, 0), iota(shape, 1)
    waves = wave(row // part_rows * HALF + row % HALF, row // HALF % 2, col)
    point = (lax.axis_index(RCV) * 2 + core) * part_focal + iota((2 * part_rows, focal), 0) // ROWS % part_focal
    block = point // focal_here
    far = sum(jnp.where(block % zh == j, f, 0) for j, f in enumerate(far_order(zh)))
    point = (far * pairs + block // zh) * focal_here + point % focal_here
    window = jnp.where(point == iota((2 * part_rows, focal), 1), gates[None, :], 0).sum(1)
    inner = jnp.where(col < window[:, None], waves / math.sqrt(NT), 0.0)
    matrix = lax.dot_general(
        inner, waves * (2.0 / math.sqrt(NT)), (((1,), (1,)), ((), ())), precision=HIGHEST
    )
    shape = matrix.shape
    same = iota(shape, 0) // ROWS % part_focal == iota(shape, 1) // ROWS % part_focal
    matrix = jnp.where(same, matrix, 0.0)
    near, masked, matrix = lax.optimization_barrier((near, masked, matrix))
    every = jnp.broadcast_to(near[None], (pairs, zh * own_rows, cols))
    every = lax.all_to_all(every, PAIR, 0, 0, tiled=True).reshape(focal * ROWS, cols)

    packed = part_rows * 3 // 2
    parts = vmem_call(
        forward_body,
        struct((chunks, packed, LANES), F32),
        [
            pltpu.VMEM((cols // LANES, focal * ROWS, LANES), F32),
            pltpu.VMEM((2, focal * ROWS, LANES), F32),
        ],
    )(every, masked)
    parts = lax.all_to_all(parts, RCV + ("c",), 0, 0, tiled=True)

    gated = vmem_call(gate_body, struct((chunks, packed, LANES), BF16))(matrix, parts)
    windowed = lax.all_to_all(gated, RCV + ("c",), 0, 0, tiled=True)

    sends = vmem_call(
        adjoint_body,
        struct((focal * ROWS, cols), BF16),
        [
            pltpu.VMEM((2, focal * ROWS, LANES), F32),
            pltpu.VMEM((cols // LANES, focal * ROWS, LANES), F32),
        ],
    )(windowed, masked)
    got = lax.all_to_all(sends.reshape(pairs, zh * own_rows, cols), PAIR, 0, 0, tiled=True)
    got = vmem_call(sum_body, struct((zh * own_rows, cols), BF16))(got)
    got = far_all_to_all(got.reshape(zh, own_rows, cols))
    got = vmem_call(sum_body, struct((own_rows, cols), F32))(got)
    both = lax.all_gather(got, "c", axis=0, tiled=True)

    return pl.pallas_call(
        focused_body,
        out_shape=struct((steps, focal_here, cols), BF16),
        in_specs=[pl.BlockSpec(memory_space=pltpu.VMEM)] * 2,
        out_specs=pl.BlockSpec(memory_space=pltpu.HBM),
        scratch_shapes=[pltpu.VMEM(f_time.shape, BF16), pltpu.SemaphoreType.DMA((4,))],
        compiler_params=pltpu.CompilerParams(vmem_limit_bytes=12 << 20),
    )(table, both)


def solution(mesh):
    src, rcv, frq = (mesh.shape[a] for a in ("src", "rcv", "frq"))
    devices = mesh.devices.reshape(src // 4, 2, 2, rcv // 2, 2, frq)
    return jax.shard_map(
        shards,
        mesh=Mesh(devices, SRC + RCV + ("c",)),
        in_specs=(P("c", SRC, RCV), P(None, "c", SRC, RCV), P(SRC, RCV), P()),
        out_specs=P("c", SRC, RCV),
        check_vma=False,
    )
```
